1024 devices in a mesh: sy: 32 (over y, x), sx: 32 (over z, core).
Axes of the slice: x: 4, y: 8, z: 16, core: 2. Of those that a mesh axis runs over, the one named last changes fastest.
Arguments:
- obj_delta: float32 [2, 2, 4096, 4096], P(None, None, 'sy', 'sx'), may hold values from -1.8 to 1.8
- probe_mean: float32 [2, 128, 128], replicated, may hold values from -6 to 6
- probe_basis: float32 [8, 2, 128, 128], replicated, may hold values from -4.2 to 4.2
- mode_weights: float32 [32, 32, 2, 8], P('sy', 'sx'), may hold values from -3 to 3
- positions: int32 [32, 32, 2, 2], P('sy', 'sx'), may hold values from 0 to 127
- amplitudes: float32 [32, 32, 2, 128, 128], P('sy', 'sx'), may hold values from 0 to 3
Outputs:
- obj_grad: float32 [2, 2, 4096, 4096], P(None, None, 'sy', 'sx')
- new_basis: float32 [8, 2, 128, 128], replicated
The draws below stay inside these ranges and needn't reach their ends.
Inputs may be any that keep to these rules, and one draw needn't show every extreme that they name: `positions`: offsets of each probe window's centre from its tile's first row and column.
All inputs are finite; a program needn't handle non-finite values.
Results may differ from the reference program's by a relative error of at most 0.00016.
Values sent between devices are 32-bit elements; how exact they have to be, the bound alone decides.
No kernel may reach another device: no remote copies, remote signals or barrier semaphores. Data moves between devices by JAX's collectives and lax.ppermute only.
A program may use at most 32 MiB of HBM per device.

```python
import math
import jax
import jax.numpy as jnp
from jax import lax

N = 128
K = 8
S = 2
TILE = 128
POS_DEV = 2
NY = 4096
NX = 4096
N_SY = 32
N_SX = 32


def with_ends(entries, key, low, largest):
    index_at = [jax.random.randint(jax.random.fold_in(key, axis), (), 0, length) for axis, length in enumerate(entries.shape)]
    main_axis = entries.shape.index(max(entries.shape))
    beside = index_at[:main_axis] + [(index_at[main_axis] + 1) % entries.shape[main_axis]] + index_at[main_axis + 1:]
    return entries.at[tuple(index_at)].set(low).at[tuple(beside)].set(largest)


def level_of(stream_key, shape, shards, least, top_value):
    gain, own = 1.0, jax.random.fold_in(stream_key, 6)
    for dim, parts in shards:
        heights = jnp.exp(jax.random.uniform(jax.random.fold_in(own, dim), (parts,), jnp.float32, least / len(shards), top_value / len(shards)))
        gain = gain * jnp.repeat(heights, shape[dim] // parts).reshape([-1 if axis == dim else 1 for axis in range(len(shape))])
    return gain


def noise(key, shape, deviation, reach, cuts=(), kind=jnp.bfloat16):
    factor_of = level_of(key, shape, cuts, -0.22, 0.18) if cuts else 1.0
    entries = jax.random.normal(key, shape, jnp.float32) * deviation * factor_of
    return jnp.minimum(jnp.maximum(entries, -reach), reach).astype(kind)


def setup_inputs(seed: int = 0) -> dict:
    keys = jax.random.split(jax.random.key(seed), 7)
    return {
        "obj_delta": noise(keys[0], (S, 2, NY, NX), 0.3, 1.8, ((2, 32), (3, 32)), jnp.float32),
        "probe_mean": noise(keys[1], (2, N, N), 1.0, 6.0, (), jnp.float32),
        "probe_basis": noise(keys[2], (K, 2, N, N), 0.7, 4.2, (), jnp.float32),
        "mode_weights": noise(keys[3], (N_SY, N_SX, POS_DEV, K), 0.5, 3.0, ((0, 32), (1, 32)), jnp.float32),
        "positions": with_ends(jax.random.randint(keys[4], (N_SY, N_SX, POS_DEV, 2), 0, TILE), jax.random.fold_in(keys[4], 1), 0, TILE - 1).astype(jnp.int32),
        "amplitudes": jnp.clip(3.0 * jax.random.uniform(keys[5], (N_SY, N_SX, POS_DEV, N, N), jnp.float32) ** level_of(keys[5], (N_SY, N_SX, POS_DEV, N, N), ((0, 32), (1, 32)), -0.2, 0.2), 0.0, 3.0),
    }


FLOOR = 0.5
PHASE_EDGE = 3.0

def propagator(probe_len):
    shifted = (jnp.arange(probe_len, dtype=jnp.int32) + probe_len // 2) % probe_len - probe_len // 2
    frequency = shifted.astype(jnp.float32) / (probe_len // 2)
    phases = PHASE_EDGE * (frequency[:, None] * frequency[:, None] + frequency[None, :] * frequency[None, :])
    return (jnp.cos(phases), -jnp.sin(phases))

def orthonormal(vec_real, vec_imag, count):
    highest = lax.Precision.HIGHEST
    gram_real = (jnp.dot(vec_real, vec_real.T, precision=highest) + jnp.dot(vec_imag, vec_imag.T, precision=highest)) / count
    gram_imag = (jnp.dot(vec_real, vec_imag.T, precision=highest) - jnp.dot(vec_imag, vec_real.T, precision=highest)) / count
    modes = vec_real.shape[0]
    upper_real = [[None] * modes for unused in range(modes)]
    upper_imag = [[None] * modes for unused in range(modes)]
    for row_at in range(modes):
        total_diag = gram_real[row_at, row_at]
        for inner in range(row_at):
            total_diag = total_diag - upper_real[inner][row_at] * upper_real[inner][row_at] - upper_imag[inner][row_at] * upper_imag[inner][row_at]
        pivot = jnp.sqrt(total_diag)
        upper_real[row_at][row_at] = pivot
        upper_imag[row_at][row_at] = jnp.zeros_like(pivot)
        for column_at in range(row_at + 1, modes):
            entry_real = gram_real[row_at, column_at]
            entry_imag = gram_imag[row_at, column_at]
            for inner in range(row_at):
                left_real = upper_real[inner][row_at]
                left_imag = upper_imag[inner][row_at]
                right_real = upper_real[inner][column_at]
                right_imag = upper_imag[inner][column_at]
                entry_real = entry_real - (left_real * right_real + left_imag * right_imag)
                entry_imag = entry_imag - (left_real * right_imag - left_imag * right_real)
            upper_real[row_at][column_at] = entry_real / pivot
            upper_imag[row_at][column_at] = entry_imag / pivot
    result_real = []
    result_imag = []
    for column_at in range(modes):
        total_real = vec_real[column_at]
        total_imag = vec_imag[column_at]
        for inner in range(column_at):
            factor_real = upper_real[inner][column_at]
            factor_imag = upper_imag[inner][column_at]
            total_real = total_real - (factor_real * result_real[inner] - factor_imag * result_imag[inner])
            total_imag = total_imag - (factor_real * result_imag[inner] + factor_imag * result_real[inner])
        pivot = upper_real[column_at][column_at]
        result_real.append(total_real / pivot)
        result_imag.append(total_imag / pivot)
    return (jnp.stack(result_real), jnp.stack(result_imag))

def reference(obj_delta, probe_mean, probe_basis, mode_weights, positions, amplitudes):
    highest = lax.Precision.HIGHEST
    slice_count = obj_delta.shape[0]
    probe_len = probe_mean.shape[-1]
    half_len = probe_len // 2
    tiles_down = positions.shape[0]
    tiles_across = positions.shape[1]
    tile_len = obj_delta.shape[2] // tiles_down
    modes = probe_basis.shape[0]
    total_count = tiles_down * tiles_across * positions.shape[2]
    block_len = math.gcd(total_count, 64)
    block_count = total_count // block_len
    kernel_real, kernel_imag = propagator(probe_len)
    kernel = lax.complex(kernel_real, kernel_imag)
    field = lax.complex(obj_delta[:, 0], obj_delta[:, 1])
    padded = jnp.pad(field, ((0, 0), (half_len, half_len), (half_len, half_len)))
    anchor_rows = (jnp.arange(tiles_down, dtype=jnp.int32) * tile_len)[:, None, None]
    anchor_cols = (jnp.arange(tiles_across, dtype=jnp.int32) * tile_len)[None, :, None]
    start_rows = (positions[..., 0] + anchor_rows).reshape(block_count, block_len)
    start_cols = (positions[..., 1] + anchor_cols).reshape(block_count, block_len)
    weights = mode_weights.reshape(block_count, block_len, modes)
    measured = amplitudes.reshape(block_count, block_len, probe_len, probe_len)
    basis = lax.complex(probe_basis[:, 0], probe_basis[:, 1])
    mean_probe = lax.complex(probe_mean[0], probe_mean[1])
    offsets = jnp.arange(probe_len, dtype=jnp.int32)

    def one_block(carry, inputs):
        grid_grad, basis_grad = carry
        rows_here, cols_here, weights_here, measured_here = inputs
        row_index = rows_here[:, None, None] + offsets[None, :, None]
        col_index = cols_here[:, None, None] + offsets[None, None, :]
        windows = padded[:, row_index, col_index]
        transmit = 1.0 + windows
        probes = mean_probe[None] + jnp.einsum('pk,kij->pij', weights_here.astype(basis.dtype), basis, precision=highest)
        wave = probes
        entering = []
        for layer in range(slice_count):
            if layer > 0:
                wave = jnp.fft.ifft2(kernel * jnp.fft.fft2(wave, norm='ortho'), norm='ortho')
            entering.append(wave)
            wave = wave * transmit[layer]
        far = jnp.fft.fft2(wave, norm='ortho')
        modulus = jnp.maximum(jnp.abs(far), FLOOR)
        back = jnp.fft.ifft2(far - measured_here * far / modulus, norm='ortho')
        slice_grads = [None] * slice_count
        for layer in range(slice_count - 1, -1, -1):
            slice_grads[layer] = jnp.conj(entering[layer]) * back
            back = jnp.conj(transmit[layer]) * back
            if layer > 0:
                back = jnp.fft.ifft2(jnp.conj(kernel) * jnp.fft.fft2(back, norm='ortho'), norm='ortho')
        grid_grad = grid_grad.at[:, row_index, col_index].add(jnp.stack(slice_grads))
        basis_grad = basis_grad + jnp.einsum('pk,pij->kij', weights_here.astype(back.dtype), back, precision=highest)
        return ((grid_grad, basis_grad), None)
    start_carry = (jnp.zeros(padded.shape, padded.dtype), jnp.zeros(basis.shape, basis.dtype))
    (grid_grad, basis_grad), unused = lax.scan(one_block, start_carry, (start_rows, start_cols, weights, measured))
    inner_grad = grid_grad[:, half_len:half_len + obj_delta.shape[2], half_len:half_len + obj_delta.shape[3]]
    obj_grad = jnp.stack([jnp.real(inner_grad), jnp.imag(inner_grad)], axis=1)
    step_len = 1.0 / math.sqrt(total_count)
    updated = basis - step_len * basis_grad
    flat_real = jnp.real(updated).reshape(modes, -1)
    flat_imag = jnp.imag(updated).reshape(modes, -1)
    new_real, new_imag = orthonormal(flat_real, flat_imag, probe_len * probe_len)
    new_basis = jnp.stack([new_real, new_imag], axis=1).reshape(probe_basis.shape)
    return (obj_grad, new_basis)
```

```python
import math

import jax
import jax.numpy as jnp
import numpy as np
from jax import lax
from jax.experimental import pallas as pl
from jax.experimental.pallas import tpu as pltpu
from jax.sharding import PartitionSpec as P

FLOOR = 0.5
PHASE_EDGE = 3.0
VMEM_BYTES = 40 * 1024 * 1024


def block_form(matrix):
    real, imag = matrix.real, matrix.imag
    return np.block([[real, -imag], [imag, real]])


def split_table(values):
    whole = values.astype(np.float32)
    high = whole.astype(jnp.bfloat16)
    low = (whole - high.astype(np.float32)).astype(jnp.bfloat16)
    return (high, low)


def tables(probe_len):
    indices = np.arange(probe_len)
    dft = np.exp(-2j * np.pi * (np.outer(indices, indices) % probe_len) / probe_len)
    dft = dft / math.sqrt(probe_len)
    half = probe_len // 2
    frequency = ((indices + half) % probe_len - half) / half
    phase = np.exp(-1j * PHASE_EDGE * frequency * frequency)
    move = np.conj(dft) @ (phase[:, None] * dft)
    forms = (block_form(dft), block_form(dft).T, block_form(move), block_form(move).T)
    parts = [split_table(form) for form in forms]
    return np.stack([np.stack(pair) for pair in parts])


def dot3(left, right):
    left_high, left_low = left
    right_high, right_low = right
    total = jnp.dot(left_high, right_low, preferred_element_type=jnp.float32)
    total = total + jnp.dot(left_low, right_high, preferred_element_type=jnp.float32)
    return total + jnp.dot(left_high, right_high, preferred_element_type=jnp.float32)


def halves(values):
    high = values.astype(jnp.bfloat16)
    low = (values - high.astype(jnp.float32)).astype(jnp.bfloat16)
    return (high, low)


def both_sides(fields, left_table, right_table):
    (real0, imag0), (real1, imag1) = fields
    n = real0.shape[0]
    upright = jnp.concatenate(
        [jnp.concatenate([real0, real1], axis=1), jnp.concatenate([imag0, imag1], axis=1)], axis=0
    )
    upright = dot3(left_table, halves(upright))
    top, bottom = upright[:n], upright[n:]
    wide = jnp.concatenate(
        [
            jnp.concatenate([top[:, :n], bottom[:, :n]], axis=1),
            jnp.concatenate([top[:, n:], bottom[:, n:]], axis=1),
        ],
        axis=0,
    )
    wide = dot3(halves(wide), right_table)
    return [(wide[:n, :n], wide[:n, n:]), (wide[n:, :n], wide[n:, n:])]


def model_kernel(
    positions, weights, own, beside, above, below, mean, basis, measured, table,
    grad_above, grad_own, grad_below, probe_grad, frame, grads,
):
    n = mean.shape[-1]
    half = n // 2
    modes = basis.shape[0]
    frame[:, 0:half, :] = above[...]
    frame[:, half : half + n, 0:n] = own[...]
    frame[:, half : half + n, n : 2 * n] = beside[...]
    frame[:, half + n : 2 * n, :] = below[...]
    grads[...] = jnp.zeros(grads.shape, jnp.float32)
    dft, dft_t, move, move_t = [(table[at, 0], table[at, 1]) for at in range(4)]
    slots = range(2)
    rows = [positions[slot, 0] for slot in slots]
    offsets = [row & 7 for row in rows]
    bases = [pl.multiple_of(row - offset, 8) for row, offset in zip(rows, offsets)]
    tall = n + 8
    cols = [positions[slot, 1] for slot in slots]

    def window(slot, plane):
        strip = frame[plane, pl.ds(bases[slot], tall), :]
        strip = pltpu.roll(strip, (5 * half - cols[slot]) & (2 * n - 1), 1)[:, :n]
        shift = jnp.where(offsets[slot] == 0, 0, tall - offsets[slot])
        return pltpu.roll(strip, shift, 0)[:n]

    transmit = [
        [(1.0 + window(slot, 2 * layer), window(slot, 2 * layer + 1)) for slot in slots]
        for layer in range(2)
    ]
    probes = []
    for slot in slots:
        real = mean[0]
        imag = mean[1]
        for mode in range(modes):
            real = real + weights[slot, mode] * basis[mode, 0]
            imag = imag + weights[slot, mode] * basis[mode, 1]
        probes.append((real, imag))

    def times(first, second):
        return [(a * c - b * d, a * d + b * c) for (a, b), (c, d) in zip(first, second)]

    def conj_times(first, second):
        return [(a * c + b * d, a * d - b * c) for (a, b), (c, d) in zip(first, second)]

    entered = both_sides(times(probes, transmit[0]), move, move_t)
    far = both_sides(times(entered, transmit[1]), dft, dft_t)
    chi = []
    for slot in slots:
        real, imag = far[slot]
        modulus = jnp.maximum(jnp.sqrt(real * real + imag * imag), FLOOR)
        ratio = measured[slot] / modulus
        chi.append((real - real * ratio, imag - imag * ratio))
    back = both_sides(chi, dft_t, dft)

    def deposit(layer, terms):
        for slot in slots:
            for part in range(2):
                padded = jnp.concatenate(
                    [terms[slot][part], jnp.zeros((8, n), jnp.float32)], axis=0
                )
                lowered = pltpu.roll(padded, offsets[slot], 0)
                padded = jnp.concatenate(
                    [lowered, jnp.zeros((tall, n), jnp.float32)], axis=1
                )
                shifted = pltpu.roll(padded, (cols[slot] + 3 * half) & (2 * n - 1), 1)
                at = (2 * layer + part, pl.ds(bases[slot], tall), slice(None))
                grads[at] = grads[at] + shifted

    deposit(1, conj_times(entered, back))
    back = both_sides(conj_times(transmit[1], back), move_t, move)
    deposit(0, conj_times(probes, back))
    back = conj_times(transmit[0], back)
    blocks = n // 8
    for slot in slots:
        for part in range(2):
            piece = back[slot][part].reshape(blocks, 8, n)
            probe_grad[part * blocks : (part + 1) * blocks, slot] = piece
    grad_above[...] = grads[:, 0:half, :]
    grad_own[...] = grads[:, half : half + n, :]
    grad_below[...] = grads[:, half + n : 2 * n, :]


def mix_kernel(weights, gathered, mixed):
    count, per_tile = gathered.shape[0], gathered.shape[1]
    modes = mixed.shape[0]
    totals = [jnp.zeros(mixed.shape[1:], jnp.float32) for mode in range(modes)]
    for source in range(count):
        for slot in range(per_tile):
            term = gathered[source, slot]
            for mode in range(modes):
                totals[mode] = totals[mode] + weights[source, slot * modes + mode] * term
    for mode in range(modes):
        mixed[mode] = totals[mode]


def ortho_kernel(core, mine, other, basis, out, step_len=None):
    modes, blocks = out.shape[0], out.shape[1]
    part_len = blocks // 2
    some = modes // 2
    pixels = part_len * out.shape[2] * out.shape[3]
    my_base = core[0] * some
    other_base = some - my_base
    for mode in range(some):
        at = my_base + mode
        out[at] = basis[at] - step_len * mine[:, mode]
        at = other_base + mode
        out[at] = basis[at] - step_len * other[:, mode]

    def total(values):
        return jnp.sum(jnp.sum(values, axis=0), axis=(0, 1), keepdims=True)

    for mode in range(modes):
        real = out[mode, 0:part_len]
        imag = out[mode, part_len:blocks]
        norm = total(real * real + imag * imag)
        for later in range(mode + 1, modes):
            later_real = out[later, 0:part_len]
            later_imag = out[later, part_len:blocks]
            factor_real = (total(real * later_real + imag * later_imag) / norm)[None]
            factor_imag = (total(real * later_imag - imag * later_real) / norm)[None]
            out[later, 0:part_len] = later_real - (factor_real * real - factor_imag * imag)
            out[later, part_len:blocks] = later_imag - (factor_real * imag + factor_imag * real)
        scale = (1.0 / jnp.sqrt(norm / pixels))[None]
        out[mode, 0:part_len] = real * scale
        out[mode, part_len:blocks] = imag * scale


def shift_pairs(count):
    forward = [(at, at + 1) for at in range(count - 1)]
    return forward, [(target, source) for source, target in forward]


def exchange(values, axis, groups=None):
    return lax.all_to_all(values, axis, 0, 0, tiled=True, axis_index_groups=groups)


def to_all(values, axis, count, groups=None):
    repeated = jnp.broadcast_to(values[None], (count,) + values.shape)
    return exchange(repeated, axis, groups)


def vmem_specs(count):
    return [pl.BlockSpec(memory_space=pltpu.VMEM)] * count


def local(obj_delta, probe_mean, probe_basis, mode_weights, positions, amplitudes):
    n = probe_mean.shape[-1]
    half = n // 2
    modes = probe_basis.shape[0]
    per_tile = positions.shape[2]
    count_y, count_x = lax.axis_size("sy"), lax.axis_size("sx")
    forward_y, backward_y = shift_pairs(count_y)
    forward_x, backward_x = shift_pairs(count_x)
    planes = obj_delta.shape[0] * obj_delta.shape[1]
    blocks = n // 8
    params = pltpu.CompilerParams(vmem_limit_bytes=VMEM_BYTES)
    smem = pl.BlockSpec(memory_space=pltpu.SMEM)
    weights = mode_weights[0, 0]

    own = obj_delta.reshape(planes, n, n)
    left = lax.ppermute(own, "sx", forward_x)
    right = lax.ppermute(own, "sx", backward_x)
    near = lax.broadcasted_iota(jnp.int32, (1, 1, n), 2) < half
    beside = jnp.where(near, right, left)
    strip = jnp.concatenate([own, beside], axis=2)
    above = lax.ppermute(strip[:, half:], "sy", forward_y)
    below = lax.ppermute(strip[:, :half], "sy", backward_y)

    flat_weights = jnp.pad(weights.reshape(1, per_tile * modes), ((0, 0), (0, 128 - per_tile * modes)))
    all_weights = to_all(flat_weights, "sy", count_y).reshape(count_y, 128)

    f32 = jnp.float32
    grad_above, grad_own, grad_below, probe_grad = pl.pallas_call(
        model_kernel,
        out_shape=(
            jax.ShapeDtypeStruct((planes, half, 2 * n), f32),
            jax.ShapeDtypeStruct((planes, n, 2 * n), f32),
            jax.ShapeDtypeStruct((planes, half, 2 * n), f32),
            jax.ShapeDtypeStruct((2 * blocks, per_tile, 8, n), f32),
        ),
        in_specs=[smem, smem] + vmem_specs(8),
        out_specs=tuple(vmem_specs(4)),
        scratch_shapes=[pltpu.VMEM((planes, 2 * n, 2 * n), f32)] * 2,
        compiler_params=params,
        name="model",
    )(
        positions[0, 0], weights, own, beside, above, below, probe_mean, probe_basis,
        amplitudes[0, 0], jnp.asarray(tables(n)),
    )

    gathered = exchange(probe_grad, "sy")
    mixed = pl.pallas_call(
        mix_kernel,
        out_shape=jax.ShapeDtypeStruct((modes, 8, n), f32),
        in_specs=[smem] + vmem_specs(1),
        out_specs=vmem_specs(1)[0],
        compiler_params=params,
        name="mix",
    )(all_weights, gathered)

    cores = 2
    per_core = count_x // cores
    pairs = [[cores * at + core for core in range(cores)] for at in range(per_core)]
    columns = [[cores * at + core for at in range(per_core)] for core in range(cores)]
    some = modes // cores
    mine = exchange(mixed, "sx", pairs).reshape(cores, some, 8, n).sum(axis=0)
    mine = to_all(mine, "sx", per_core, columns).sum(axis=0)
    mine = to_all(mine, "sy", count_y)
    swap = [(at, at ^ 1) for at in range(count_x)]
    other = lax.ppermute(mine, "sx", swap)
    core = (lax.axis_index("sx") % cores).astype(jnp.int32).reshape(1)
    count_all = per_tile * count_y * count_x
    step_len = 1.0 / math.sqrt(count_all)

    def final_kernel(*refs):
        ortho_kernel(*refs, step_len=step_len)

    new_basis = pl.pallas_call(
        final_kernel,
        out_shape=jax.ShapeDtypeStruct((modes, 2 * blocks, 8, n), f32),
        in_specs=[smem] + vmem_specs(3),
        out_specs=vmem_specs(1)[0],
        compiler_params=params,
        name="orthonormal",
    )(core, mine, other, probe_basis.reshape(modes, 2 * blocks, 8, n))
    new_basis = new_basis.reshape(probe_basis.shape)

    from_below = lax.ppermute(grad_above, "sy", backward_y)
    from_above = lax.ppermute(grad_below, "sy", forward_y)
    joined = grad_own + jnp.concatenate([from_above, from_below], axis=1)
    outer = joined[:, :, n:]
    from_left = lax.ppermute(outer, "sx", forward_x)
    from_right = lax.ppermute(outer, "sx", backward_x)
    obj_grad = joined[:, :, :n] + jnp.where(near, from_left, from_right)
    return (obj_grad.reshape(obj_delta.shape), new_basis)


def solution(mesh):
    placed = (
        P(None, None, "sy", "sx"),
        P(),
        P(),
        P("sy", "sx", None, None),
        P("sy", "sx", None, None),
        P("sy", "sx", None, None, None),
    )
    return jax.shard_map(
        local,
        mesh=mesh,
        in_specs=placed,
        out_specs=(P(None, None, "sy", "sx"), P()),
        check_vma=False,
    )
```

```python
import math

import jax
import jax.numpy as jnp
import numpy as np
from jax import lax
from jax.experimental import pallas as pl
from jax.experimental.pallas import tpu as pltpu
from jax.sharding import PartitionSpec as P

FLOOR = 0.5
PHASE_EDGE = 3.0
VMEM_BYTES = 40 * 1024 * 1024


def split_table(values):
    whole = values.astype(np.float32)
    high = whole.astype(jnp.bfloat16)
    low = (whole - high.astype(np.float32)).astype(jnp.bfloat16)
    return np.stack([high, low])


def tables(probe_len):
    indices = np.arange(probe_len)
    dft = np.exp(-2j * np.pi * (np.outer(indices, indices) % probe_len) / probe_len)
    dft = dft / math.sqrt(probe_len)
    half = probe_len // 2
    frequency = ((indices + half) % probe_len - half) / half
    phase = np.exp(-1j * PHASE_EDGE * frequency * frequency)
    move = np.conj(dft) @ (phase[:, None] * dft)
    parts = [split_table(part) for form in (dft, move) for part in (form.real, form.imag)]
    return np.stack(parts)


def block_forms(real, imag):
    above = jnp.concatenate([real, -imag], axis=1)
    below = jnp.concatenate([imag, real], axis=1)
    above_t = jnp.concatenate([real, imag], axis=1)
    below_t = jnp.concatenate([-imag, real], axis=1)
    return (
        jnp.concatenate([above, below], axis=0),
        jnp.concatenate([above_t, below_t], axis=0),
    )


def dot3(left, right):
    left_high, left_low = left
    right_high, right_low = right
    total = jnp.dot(left_high, right_low, preferred_element_type=jnp.float32)
    total = total + jnp.dot(left_low, right_high, preferred_element_type=jnp.float32)
    return total + jnp.dot(left_high, right_high, preferred_element_type=jnp.float32)


def halves(values):
    high = values.astype(jnp.bfloat16)
    low = (values - high.astype(jnp.float32)).astype(jnp.bfloat16)
    return (high, low)


def both_sides(fields, left_table, right_table):
    (real0, imag0), (real1, imag1) = fields
    n = real0.shape[0]
    upright = jnp.concatenate(
        [jnp.concatenate([real0, real1], axis=1), jnp.concatenate([imag0, imag1], axis=1)], axis=0
    )
    upright = dot3(left_table, halves(upright))
    top, bottom = upright[:n], upright[n:]
    wide = jnp.concatenate(
        [
            jnp.concatenate([top[:, :n], bottom[:, :n]], axis=1),
            jnp.concatenate([top[:, n:], bottom[:, n:]], axis=1),
        ],
        axis=0,
    )
    wide = dot3(halves(wide), right_table)
    return [(wide[:n, :n], wide[:n, n:]), (wide[n:, :n], wide[n:, n:])]


def near_lanes(shape):
    return lax.broadcasted_iota(jnp.int32, shape, len(shape) - 1) < shape[-1] // 2


def roll_planes(values):
    return jnp.stack([pltpu.roll(plane, plane.shape[-1] // 2, 1) for plane in values])


def split_kernel(source, own, upper, lower, sems):
    half = upper.shape[1]
    copies = [
        pltpu.make_async_copy(source.at[:, 0:half], upper, sems.at[0]),
        pltpu.make_async_copy(source.at[:, half : 2 * half], lower, sems.at[1]),
        pltpu.make_async_copy(source, own, sems.at[2]),
    ]
    for copy in copies:
        copy.start()
    for copy in copies:
        copy.wait()


def repeat_kernel(parts, out):
    total = parts[0]
    for at in range(1, parts.shape[0]):
        total = total + parts[at]
    for at in range(out.shape[0]):
        out[at] = total


def pack_kernel(own, above, below, to_left, to_right):
    n = own.shape[-1]
    half = n // 2
    near = near_lanes(own.shape)
    first = jnp.concatenate([above[...], own[:, :half]], axis=1)
    second = jnp.concatenate([own[:, half:], below[...]], axis=1)
    second = roll_planes(second)
    to_left[...] = jnp.where(near, first, second)
    to_right[...] = jnp.where(near, second, first)


def merge_kernel(tall, from_left, from_right, up, middle, down):
    n = tall.shape[-1]
    half = n // 2
    near = near_lanes(from_left.shape)
    first = tall[:, :n] + jnp.where(near, from_left[...], from_right[...])
    second = tall[:, n:] + roll_planes(jnp.where(near, from_right[...], from_left[...]))
    up[...] = first[:, :half]
    middle[:, :half] = first[:, half:]
    middle[:, half:] = second[:, :half]
    down[...] = second[:, half:]


def model_kernel(
    positions_in, weights, own, above, below, from_left, from_right, mean_in, basis_in,
    measured_in, table_in, tall, to_left, to_right, probe_grad,
    frame, grads, positions, mean, basis, measured, table, sems,
):
    copies = [
        pltpu.make_async_copy(source, target, sems.at[at])
        for at, (source, target) in enumerate(
            [
                (positions_in, positions),
                (mean_in, mean),
                (basis_in, basis),
                (table_in, table),
                (measured_in, measured),
            ]
        )
    ]
    for copy in copies:
        copy.start()
    n = mean.shape[-1]
    half = n // 2
    modes = basis.shape[0]
    near = near_lanes(own.shape)
    frame[:, 0:half, 0:n] = above[...]
    frame[:, half : half + n, 0:n] = own[...]
    frame[:, half + n : 2 * n, 0:n] = below[...]
    frame[:, 0:n, n : 2 * n] = jnp.where(near, from_right[...], from_left[...])
    frame[:, n : 2 * n, n : 2 * n] = roll_planes(
        jnp.where(near, from_left[...], from_right[...])
    )
    grads[...] = jnp.zeros(grads.shape, jnp.float32)
    slots = range(2)
    copies[0].wait()
    rows = [positions[slot, 0] for slot in slots]
    offsets = [row & 7 for row in rows]
    bases = [pl.multiple_of(row - offset, 8) for row, offset in zip(rows, offsets)]
    span = n + 8
    cols = [positions[slot, 1] for slot in slots]

    def window(slot, plane):
        strip = frame[plane, pl.ds(bases[slot], span), :]
        strip = pltpu.roll(strip, (5 * half - cols[slot]) & (2 * n - 1), 1)[:, :n]
        shift = jnp.where(offsets[slot] == 0, 0, span - offsets[slot])
        return pltpu.roll(strip, shift, 0)[:n]

    transmit = [
        [(1.0 + window(slot, 2 * layer), window(slot, 2 * layer + 1)) for slot in slots]
        for layer in range(2)
    ]
    copies[1].wait()
    copies[2].wait()
    probes = []
    for slot in slots:
        real = mean[0]
        imag = mean[1]
        for mode in range(modes):
            real = real + weights[slot, mode] * basis[mode, 0]
            imag = imag + weights[slot, mode] * basis[mode, 1]
        probes.append((real, imag))

    def times(first, second):
        return [(a * c - b * d, a * d + b * c) for (a, b), (c, d) in zip(first, second)]

    def conj_times(first, second):
        return [(a * c + b * d, a * d - b * c) for (a, b), (c, d) in zip(first, second)]

    copies[3].wait()
    dft_high, dft_t_high = block_forms(table[0, 0], table[1, 0])
    dft_low, dft_t_low = block_forms(table[0, 1], table[1, 1])
    move_high, move_t_high = block_forms(table[2, 0], table[3, 0])
    move_low, move_t_low = block_forms(table[2, 1], table[3, 1])
    dft, dft_t = (dft_high, dft_low), (dft_t_high, dft_t_low)
    move, move_t = (move_high, move_low), (move_t_high, move_t_low)
    entered = both_sides(times(probes, transmit[0]), move, move_t)
    far = both_sides(times(entered, transmit[1]), dft, dft_t)
    copies[4].wait()
    chi = []
    for slot in slots:
        real, imag = far[slot]
        modulus = jnp.maximum(jnp.sqrt(real * real + imag * imag), FLOOR)
        ratio = measured[slot] / modulus
        chi.append((real - real * ratio, imag - imag * ratio))
    back = both_sides(chi, dft_t, dft)

    def deposit(layer, terms):
        for slot in slots:
            for part in range(2):
                padded = jnp.concatenate(
                    [terms[slot][part], jnp.zeros((8, n), jnp.float32)], axis=0
                )
                lowered = pltpu.roll(padded, offsets[slot], 0)
                padded = jnp.concatenate(
                    [lowered, jnp.zeros((span, n), jnp.float32)], axis=1
                )
                shifted = pltpu.roll(padded, (cols[slot] + 3 * half) & (2 * n - 1), 1)
                at = (2 * layer + part, pl.ds(bases[slot], span), slice(None))
                grads[at] = grads[at] + shifted

    deposit(1, conj_times(entered, back))
    back = both_sides(conj_times(transmit[1], back), move_t, move)
    deposit(0, conj_times(probes, back))
    back = conj_times(transmit[0], back)
    blocks = n // 8
    for slot in slots:
        for part in range(2):
            piece = back[slot][part].reshape(blocks, 8, n)
            probe_grad[part * blocks : (part + 1) * blocks, slot] = piece
    row_at = lax.broadcasted_iota(jnp.int32, (modes, n), 0)
    lane_at = lax.broadcasted_iota(jnp.int32, (modes, n), 1)
    packed = jnp.zeros((modes, n), jnp.float32)
    for slot in slots:
        for mode in range(modes):
            here = (row_at == mode) & ((lane_at >= half) == (slot == 1))
            packed = jnp.where(here, weights[slot, mode], packed)
    probe_grad[:, 2] = jnp.broadcast_to(packed[None], (2 * blocks, modes, n))
    tall[...] = grads[:, :, 0:n]
    first = grads[:, 0:n, n : 2 * n]
    second = roll_planes(grads[:, n : 2 * n, n : 2 * n])
    to_right[...] = jnp.where(near, first, second)
    to_left[...] = jnp.where(near, second, first)


def mix_kernel(gathered, mixed):
    count, per_tile = gathered.shape[0], gathered.shape[1] - 1
    modes, rows, n = mixed.shape
    totals = [jnp.zeros((modes, n), jnp.float32) for row in range(rows)]
    for source in range(count):
        packed = gathered[source, per_tile]
        for slot in range(per_tile):
            lane = slot * (n // 2)
            factor = jnp.broadcast_to(packed[:, lane : lane + 1], (modes, n))
            for row in range(rows):
                term = gathered[source, slot, row : row + 1]
                totals[row] = totals[row] + factor * term
    for row in range(rows):
        mixed[:, row] = totals[row]


def ortho_kernel(core, mine, other, basis, out, step_len=None):
    modes, blocks = out.shape[0], out.shape[1]
    part_len = blocks // 2
    some = modes // 2
    pixels = part_len * out.shape[2] * out.shape[3]
    my_base = core[0] * some
    other_base = some - my_base
    for mode in range(some):
        at = my_base + mode
        out[at] = basis[at] - step_len * mine[:, mode]
        at = other_base + mode
        out[at] = basis[at] - step_len * other[:, mode]

    def total(values):
        return jnp.sum(jnp.sum(values, axis=0), axis=(0, 1), keepdims=True)

    for mode in range(modes):
        real = out[mode, 0:part_len]
        imag = out[mode, part_len:blocks]
        norm = total(real * real + imag * imag)
        for later in range(mode + 1, modes):
            later_real = out[later, 0:part_len]
            later_imag = out[later, part_len:blocks]
            factor_real = (total(real * later_real + imag * later_imag) / norm)[None]
            factor_imag = (total(real * later_imag - imag * later_real) / norm)[None]
            out[later, 0:part_len] = later_real - (factor_real * real - factor_imag * imag)
            out[later, part_len:blocks] = later_imag - (factor_real * imag + factor_imag * real)
        scale = (1.0 / jnp.sqrt(norm / pixels))[None]
        out[mode, 0:part_len] = real * scale
        out[mode, part_len:blocks] = imag * scale


def shift_pairs(count):
    forward = [(at, at + 1) for at in range(count - 1)]
    return forward, [(target, source) for source, target in forward]


def exchange(values, axis, groups=None):
    return lax.all_to_all(values, axis, 0, 0, tiled=True, axis_index_groups=groups)


def away(values):
    return pltpu.with_memory_space_constraint(values, pltpu.HBM)


def vmem_specs(count):
    return [pl.BlockSpec(memory_space=pltpu.VMEM)] * count


def local(obj_delta, probe_mean, probe_basis, mode_weights, positions, amplitudes):
    n = probe_mean.shape[-1]
    half = n // 2
    modes = probe_basis.shape[0]
    per_tile = positions.shape[2]
    count_y, count_x = lax.axis_size("sy"), lax.axis_size("sx")
    forward_y, backward_y = shift_pairs(count_y)
    forward_x, backward_x = shift_pairs(count_x)
    planes = obj_delta.shape[0] * obj_delta.shape[1]
    blocks = n // 8
    params = pltpu.CompilerParams(vmem_limit_bytes=VMEM_BYTES)
    smem = pl.BlockSpec(memory_space=pltpu.SMEM)
    weights = mode_weights[0, 0]

    f32 = jnp.float32
    block = jax.ShapeDtypeStruct((planes, n, n), f32)
    edge = jax.ShapeDtypeStruct((planes, half, n), f32)
    distant = pl.BlockSpec(memory_space=pltpu.HBM)
    own, upper, lower = pl.pallas_call(
        split_kernel,
        out_shape=(block, edge, edge),
        in_specs=[distant],
        out_specs=tuple(vmem_specs(3)),
        scratch_shapes=[pltpu.SemaphoreType.DMA((3,))],
        compiler_params=params,
        name="split",
    )(away(obj_delta.reshape(planes, n, n)))
    above = lax.ppermute(lower, "sy", forward_y)
    below = lax.ppermute(upper, "sy", backward_y)
    to_left, to_right = pl.pallas_call(
        pack_kernel,
        out_shape=(block, block),
        in_specs=vmem_specs(3),
        out_specs=tuple(vmem_specs(2)),
        compiler_params=params,
        name="pack",
    )(own, above, below)
    from_left = lax.ppermute(to_right, "sx", forward_x)
    from_right = lax.ppermute(to_left, "sx", backward_x)

    tall, to_left, to_right, probe_grad = pl.pallas_call(
        model_kernel,
        out_shape=(
            jax.ShapeDtypeStruct((planes, 2 * n, n), f32),
            block,
            block,
            jax.ShapeDtypeStruct((2 * blocks, per_tile + 1, 8, n), f32),
        ),
        in_specs=[distant, smem] + vmem_specs(5) + [distant] * 4,
        out_specs=tuple(vmem_specs(4)),
        scratch_shapes=[
            pltpu.VMEM((planes, 2 * n, 2 * n), f32),
            pltpu.VMEM((planes, 2 * n, 2 * n), f32),
            pltpu.SMEM((per_tile, 2), jnp.int32),
            pltpu.VMEM((2, n, n), f32),
            pltpu.VMEM((modes, 2, n, n), f32),
            pltpu.VMEM((per_tile, n, n), f32),
            pltpu.VMEM((4, 2, n, n), jnp.bfloat16),
            pltpu.SemaphoreType.DMA((5,)),
        ],
        compiler_params=params,
        name="model",
    )(
        away(positions[0, 0]), weights, own, above, below, from_left, from_right,
        away(probe_mean), away(probe_basis), away(amplitudes[0, 0]),
        away(jnp.asarray(tables(n))),
    )

    gathered = exchange(probe_grad, "sy")
    from_left = lax.ppermute(to_right, "sx", forward_x)
    from_right = lax.ppermute(to_left, "sx", backward_x)
    gathered, from_left, from_right = lax.optimization_barrier((gathered, from_left, from_right))
    mixed = pl.pallas_call(
        mix_kernel,
        out_shape=jax.ShapeDtypeStruct((modes, 8, n), f32),
        in_specs=vmem_specs(1),
        out_specs=vmem_specs(1)[0],
        compiler_params=params,
        name="mix",
    )(gathered)
    cores = 2
    per_core = count_x // cores
    pairs = [[cores * at + core for core in range(cores)] for at in range(per_core)]
    columns = [[cores * at + core for at in range(per_core)] for core in range(cores)]
    some = modes // cores
    def summed_copies(parts, count):
        return pl.pallas_call(
            repeat_kernel,
            out_shape=jax.ShapeDtypeStruct((count,) + parts.shape[1:], f32),
            in_specs=vmem_specs(1),
            out_specs=vmem_specs(1)[0],
            compiler_params=params,
            name="repeat",
        )(parts)

    parts = exchange(mixed, "sx", pairs).reshape(cores, some, 8, n)
    parts = exchange(summed_copies(parts, per_core), "sx", columns)
    up, middle, down = pl.pallas_call(
        merge_kernel,
        out_shape=(edge, block, edge),
        in_specs=vmem_specs(3),
        out_specs=tuple(vmem_specs(3)),
        compiler_params=params,
        name="merge",
    )(tall, from_left, from_right)
    from_below = lax.ppermute(up, "sy", backward_y)
    from_above = lax.ppermute(down, "sy", forward_y)
    parts, from_below, from_above = lax.optimization_barrier((parts, from_below, from_above))
    mine = exchange(summed_copies(parts, count_y), "sy")
    swap = [(at, at ^ 1) for at in range(count_x)]
    other = lax.ppermute(mine, "sx", swap)
    core = (lax.axis_index("sx") % cores).astype(jnp.int32).reshape(1)
    count_all = per_tile * count_y * count_x
    step_len = 1.0 / math.sqrt(count_all)

    def final_kernel(*refs):
        ortho_kernel(*refs, step_len=step_len)

    new_basis = pl.pallas_call(
        final_kernel,
        out_shape=jax.ShapeDtypeStruct((modes, 2 * blocks, 8, n), f32),
        in_specs=[smem] + vmem_specs(3),
        out_specs=vmem_specs(1)[0],
        compiler_params=params,
        name="orthonormal",
    )(core, mine, other, probe_basis.reshape(modes, 2 * blocks, 8, n))
    new_basis = new_basis.reshape(probe_basis.shape)

    obj_grad = middle + jnp.concatenate([from_above, from_below], axis=1)
    return (obj_grad.reshape(obj_delta.shape), new_basis)


def solution(mesh):
    placed = (
        P(None, None, "sy", "sx"),
        P(),
        P(),
        P("sy", "sx", None, None),
        P("sy", "sx", None, None),
        P("sy", "sx", None, None, None),
    )
    return jax.shard_map(
        local,
        mesh=mesh,
        in_specs=placed,
        out_specs=(P(None, None, "sy", "sx"), P()),
        check_vma=False,
    )
```

```python
import math

import jax
import jax.numpy as jnp
import numpy as np
from jax import lax
from jax.experimental import pallas as pl
from jax.experimental.pallas import tpu as pltpu
from jax.sharding import PartitionSpec as P

FLOOR = 0.5
PHASE_EDGE = 3.0
VMEM_BYTES = 40 * 1024 * 1024
PIECE = 9


def split_table(values):
    whole = values.astype(np.float32)
    high = whole.astype(jnp.bfloat16)
    low = (whole - high.astype(np.float32)).astype(jnp.bfloat16)
    return np.stack([high, low])


def tables(probe_len):
    indices = np.arange(probe_len)
    dft = np.exp(-2j * np.pi * (np.outer(indices, indices) % probe_len) / probe_len)
    dft = dft / math.sqrt(probe_len)
    half = probe_len // 2
    frequency = ((indices + half) % probe_len - half) / half
    phase = np.exp(-1j * PHASE_EDGE * frequency * frequency)
    move = np.conj(dft) @ (phase[:, None] * dft)
    parts = [split_table(part) for form in (dft, move) for part in (form.real, form.imag)]
    return np.stack(parts)


def block_forms(real, imag):
    above = jnp.concatenate([real, -imag], axis=1)
    below = jnp.concatenate([imag, real], axis=1)
    above_t = jnp.concatenate([real, imag], axis=1)
    below_t = jnp.concatenate([-imag, real], axis=1)
    return (
        jnp.concatenate([above, below], axis=0),
        jnp.concatenate([above_t, below_t], axis=0),
    )


def dot3(left, right):
    left_high, left_low = left
    right_high, right_low = right
    total = jnp.dot(left_high, right_low, preferred_element_type=jnp.float32)
    total = total + jnp.dot(left_low, right_high, preferred_element_type=jnp.float32)
    return total + jnp.dot(left_high, right_high, preferred_element_type=jnp.float32)


def halves(values):
    high = values.astype(jnp.bfloat16)
    low = (values - high.astype(jnp.float32)).astype(jnp.bfloat16)
    return (high, low)


def both_sides(fields, left_table, right_table):
    (real0, imag0), (real1, imag1) = fields
    n = real0.shape[0]
    upright = jnp.concatenate(
        [jnp.concatenate([real0, real1], axis=1), jnp.concatenate([imag0, imag1], axis=1)], axis=0
    )
    upright = dot3(left_table, halves(upright))
    top, bottom = upright[:n], upright[n:]
    wide = jnp.concatenate(
        [
            jnp.concatenate([top[:, :n], bottom[:, :n]], axis=1),
            jnp.concatenate([top[:, n:], bottom[:, n:]], axis=1),
        ],
        axis=0,
    )
    wide = dot3(halves(wide), right_table)
    return [(wide[:n, :n], wide[:n, n:]), (wide[n:, :n], wide[n:, n:])]


def near_lanes(shape):
    return lax.broadcasted_iota(jnp.int32, shape, len(shape) - 1) < shape[-1] // 2


def roll_planes(values):
    return jnp.stack([pltpu.roll(plane, plane.shape[-1] // 2, 1) for plane in values])


def split_kernel(source, own, upper, lower, sems):
    half = upper.shape[1]
    copies = [
        pltpu.make_async_copy(source.at[:, 0:half], upper, sems.at[0]),
        pltpu.make_async_copy(source.at[:, half : 2 * half], lower, sems.at[1]),
        pltpu.make_async_copy(source, own, sems.at[2]),
    ]
    for copy in copies:
        copy.start()
    for copy in copies:
        copy.wait()


def repeat_kernel(parts, out):
    total = parts[0]
    for at in range(1, parts.shape[0]):
        total = total + parts[at]
    for at in range(out.shape[0]):
        out[at] = total


def pack_kernel(own, above, below, to_left, to_right):
    n = own.shape[-1]
    half = n // 2
    near = near_lanes(own.shape)
    first = jnp.concatenate([above[...], own[:, :half]], axis=1)
    second = jnp.concatenate([own[:, half:], below[...]], axis=1)
    second = roll_planes(second)
    to_left[...] = jnp.where(near, first, second)
    to_right[...] = jnp.where(near, second, first)


def merge_kernel(tall, from_left, from_right, up, middle, down):
    n = tall.shape[-1]
    half = n // 2
    near = near_lanes(from_left.shape)
    first = tall[:, :n] + jnp.where(near, from_left[...], from_right[...])
    second = tall[:, n:] + roll_planes(jnp.where(near, from_right[...], from_left[...]))
    up[...] = first[:, :half]
    middle[:, :half] = first[:, half:]
    middle[:, half:] = second[:, :half]
    down[...] = second[:, half:]


def model_kernel(
    positions_in, weights_in, own, above, below, from_left, from_right, mean_in, basis_in,
    measured_in, table_in, tall, to_left, to_right, probe_grad,
    frame, grads, positions, weights, mean, basis, measured, table, sems,
):
    copies = [
        pltpu.make_async_copy(source, target, sems.at[at])
        for at, (source, target) in enumerate(
            [
                (positions_in, positions),
                (weights_in, weights),
                (mean_in, mean),
                (basis_in, basis),
                (table_in, table),
                (measured_in, measured),
            ]
        )
    ]
    for copy in copies:
        copy.start()
    n = mean.shape[-1]
    half = n // 2
    modes = basis.shape[0]
    near = near_lanes(own.shape)
    frame[:, 0:half, 0:n] = above[...]
    frame[:, half : half + n, 0:n] = own[...]
    frame[:, half + n : 2 * n, 0:n] = below[...]
    frame[:, 0:n, n : 2 * n] = jnp.where(near, from_right[...], from_left[...])
    frame[:, n : 2 * n, n : 2 * n] = roll_planes(
        jnp.where(near, from_left[...], from_right[...])
    )
    grads[...] = jnp.zeros(grads.shape, jnp.float32)
    slots = range(2)
    copies[0].wait()
    rows = [positions[slot, 0] for slot in slots]
    offsets = [row & 7 for row in rows]
    bases = [pl.multiple_of(row - offset, 8) for row, offset in zip(rows, offsets)]
    span = n + 8
    cols = [positions[slot, 1] for slot in slots]

    def window(slot, plane):
        strip = frame[plane, pl.ds(bases[slot], span), :]
        strip = pltpu.roll(strip, (5 * half - cols[slot]) & (2 * n - 1), 1)[:, :n]
        shift = jnp.where(offsets[slot] == 0, 0, span - offsets[slot])
        return pltpu.roll(strip, shift, 0)[:n]

    transmit = [
        [(1.0 + window(slot, 2 * layer), window(slot, 2 * layer + 1)) for slot in slots]
        for layer in range(2)
    ]
    for at in (1, 2, 3):
        copies[at].wait()
    probes = []
    for slot in slots:
        real = mean[0]
        imag = mean[1]
        for mode in range(modes):
            real = real + weights[slot, mode] * basis[mode, 0]
            imag = imag + weights[slot, mode] * basis[mode, 1]
        probes.append((real, imag))

    def times(first, second):
        return [(a * c - b * d, a * d + b * c) for (a, b), (c, d) in zip(first, second)]

    def conj_times(first, second):
        return [(a * c + b * d, a * d - b * c) for (a, b), (c, d) in zip(first, second)]

    copies[4].wait()
    dft_high, dft_t_high = block_forms(table[0, 0], table[1, 0])
    dft_low, dft_t_low = block_forms(table[0, 1], table[1, 1])
    move_high, move_t_high = block_forms(table[2, 0], table[3, 0])
    move_low, move_t_low = block_forms(table[2, 1], table[3, 1])
    dft, dft_t = (dft_high, dft_low), (dft_t_high, dft_t_low)
    move, move_t = (move_high, move_low), (move_t_high, move_t_low)
    entered = both_sides(times(probes, transmit[0]), move, move_t)
    far = both_sides(times(entered, transmit[1]), dft, dft_t)
    copies[5].wait()
    chi = []
    for slot in slots:
        real, imag = far[slot]
        modulus = jnp.maximum(jnp.sqrt(real * real + imag * imag), FLOOR)
        ratio = measured[slot] / modulus
        chi.append((real - real * ratio, imag - imag * ratio))
    back = both_sides(chi, dft_t, dft)

    def deposit(layer, terms):
        for slot in slots:
            for part in range(2):
                padded = jnp.concatenate(
                    [terms[slot][part], jnp.zeros((8, n), jnp.float32)], axis=0
                )
                lowered = pltpu.roll(padded, offsets[slot], 0)
                padded = jnp.concatenate(
                    [lowered, jnp.zeros((span, n), jnp.float32)], axis=1
                )
                shifted = pltpu.roll(padded, (cols[slot] + 3 * half) & (2 * n - 1), 1)
                at = (2 * layer + part, pl.ds(bases[slot], span), slice(None))
                grads[at] = grads[at] + shifted

    deposit(1, conj_times(entered, back))
    back = both_sides(conj_times(transmit[1], back), move_t, move)
    deposit(0, conj_times(probes, back))
    back = conj_times(transmit[0], back)
    blocks = n // 8
    upper_rows = lax.broadcasted_iota(jnp.int32, (8, n), 0) < 4
    lane_at = lax.broadcasted_iota(jnp.int32, (1, n), 1)
    packed = jnp.zeros((1, n), jnp.float32)
    for slot in slots:
        for mode in range(modes):
            packed = jnp.where(lane_at == slot * modes + mode, weights[slot, mode], packed)
    for part in range(2):
        for block in range(blocks):
            first = back[0][part][8 * block : 8 * block + 8]
            second = back[1][part][8 * block : 8 * block + 8]
            at = 2 * PIECE * (part * blocks + block)
            probe_grad[pl.ds(at, 8), 0, :] = jnp.where(
                upper_rows, first, pltpu.roll(second, 4, 0)
            )
            probe_grad[at + 8] = packed
            probe_grad[pl.ds(at + PIECE, 8), 0, :] = jnp.where(
                upper_rows, pltpu.roll(first, 4, 0), second
            )
            probe_grad[at + PIECE + 8] = packed
    tall[...] = grads[:, :, 0:n]
    first = grads[:, 0:n, n : 2 * n]
    second = roll_planes(grads[:, n : 2 * n, n : 2 * n])
    to_right[...] = jnp.where(near, first, second)
    to_left[...] = jnp.where(near, second, first)


def mix_kernel(gathered, out, ordered):
    copies, pairs, rows, n = out.shape
    modes = 2 * pairs
    some = rows // 2
    count = gathered.shape[0] // PIECE

    def row_of_all(at):
        return gathered[pl.ds(at, count, stride=PIECE), 0, :]

    factors = row_of_all(rows).T[: 2 * modes]
    terms = jnp.concatenate([row_of_all(at) for at in range(rows)], axis=1)
    product = jnp.dot(
        factors, terms, precision=lax.Precision.HIGHEST, preferred_element_type=jnp.float32
    )
    for row in range(some):
        first = product[:modes, row * n : (row + 1) * n]
        second = product[modes:, (some + row) * n : (some + row + 1) * n]
        ordered[pl.ds(row, modes, stride=some), :] = first + second
    for pair in range(pairs):
        tile = ordered[pair * rows : (pair + 1) * rows]
        for copy in range(copies):
            out[copy, pair] = tile


def ortho_kernel(core, mine, other, basis, out, step_len=None):
    modes, blocks, rows, n = out.shape
    part_len = blocks // 2
    pixels = part_len * rows * n
    upper_rows = lax.broadcasted_iota(jnp.int32, (rows, n), 0) < rows // 2
    first_core = core[0] == 0
    for block in range(blocks):
        for pair in range(modes // 2):
            low = jnp.where(first_core, mine[block, pair], other[block, pair])
            high = jnp.where(first_core, other[block, pair], mine[block, pair])
            even = jnp.where(upper_rows, low, pltpu.roll(high, rows // 2, 0))
            odd = jnp.where(upper_rows, pltpu.roll(low, rows // 2, 0), high)
            out[2 * pair, block] = basis[2 * pair, block] - step_len * even
            out[2 * pair + 1, block] = basis[2 * pair + 1, block] - step_len * odd

    def total(values):
        return jnp.sum(jnp.sum(values, axis=0), axis=(0, 1), keepdims=True)

    for mode in range(modes):
        real = out[mode, 0:part_len]
        imag = out[mode, part_len:blocks]
        norm = total(real * real + imag * imag)
        for later in range(mode + 1, modes):
            later_real = out[later, 0:part_len]
            later_imag = out[later, part_len:blocks]
            factor_real = (total(real * later_real + imag * later_imag) / norm)[None]
            factor_imag = (total(real * later_imag - imag * later_real) / norm)[None]
            out[later, 0:part_len] = later_real - (factor_real * real - factor_imag * imag)
            out[later, part_len:blocks] = later_imag - (factor_real * imag + factor_imag * real)
        scale = (1.0 / jnp.sqrt(norm / pixels))[None]
        out[mode, 0:part_len] = real * scale
        out[mode, part_len:blocks] = imag * scale


def shift_pairs(count):
    forward = [(at, at + 1) for at in range(count - 1)]
    return forward, [(target, source) for source, target in forward]


def exchange(values, axis, groups=None):
    return lax.all_to_all(values, axis, 0, 0, tiled=True, axis_index_groups=groups)


def away(values):
    return pltpu.with_memory_space_constraint(values, pltpu.HBM)


def vmem_specs(count):
    return [pl.BlockSpec(memory_space=pltpu.VMEM)] * count


def local(obj_delta, probe_mean, probe_basis, mode_weights, positions, amplitudes):
    n = probe_mean.shape[-1]
    half = n // 2
    modes = probe_basis.shape[0]
    per_tile = positions.shape[2]
    count_y, count_x = lax.axis_size("sy"), lax.axis_size("sx")
    forward_y, backward_y = shift_pairs(count_y)
    forward_x, backward_x = shift_pairs(count_x)
    planes = obj_delta.shape[0] * obj_delta.shape[1]
    blocks = n // 8
    params = pltpu.CompilerParams(vmem_limit_bytes=VMEM_BYTES)
    smem = pl.BlockSpec(memory_space=pltpu.SMEM)

    f32 = jnp.float32
    block = jax.ShapeDtypeStruct((planes, n, n), f32)
    edge = jax.ShapeDtypeStruct((planes, half, n), f32)
    distant = pl.BlockSpec(memory_space=pltpu.HBM)
    own, upper, lower = pl.pallas_call(
        split_kernel,
        out_shape=(block, edge, edge),
        in_specs=[distant],
        out_specs=tuple(vmem_specs(3)),
        scratch_shapes=[pltpu.SemaphoreType.DMA((3,))],
        compiler_params=params,
        name="split",
    )(away(obj_delta.reshape(planes, n, n)))
    above = lax.ppermute(lower, "sy", forward_y)
    below = lax.ppermute(upper, "sy", backward_y)
    to_left, to_right = pl.pallas_call(
        pack_kernel,
        out_shape=(block, block),
        in_specs=vmem_specs(3),
        out_specs=tuple(vmem_specs(2)),
        compiler_params=params,
        name="pack",
    )(own, above, below)
    from_left = lax.ppermute(to_right, "sx", forward_x)
    from_right = lax.ppermute(to_left, "sx", backward_x)

    tall, to_left, to_right, probe_grad = pl.pallas_call(
        model_kernel,
        out_shape=(
            jax.ShapeDtypeStruct((planes, 2 * n, n), f32),
            block,
            block,
            jax.ShapeDtypeStruct((4 * blocks * PIECE, 1, n), f32),
        ),
        in_specs=[distant] * 2 + vmem_specs(5) + [distant] * 4,
        out_specs=tuple(vmem_specs(4)),
        scratch_shapes=[
            pltpu.VMEM((planes, 2 * n, 2 * n), f32),
            pltpu.VMEM((planes, 2 * n, 2 * n), f32),
            pltpu.SMEM((per_tile, 2), jnp.int32),
            pltpu.SMEM((per_tile, modes), f32),
            pltpu.VMEM((2, n, n), f32),
            pltpu.VMEM((modes, 2, n, n), f32),
            pltpu.VMEM((per_tile, n, n), f32),
            pltpu.VMEM((4, 2, n, n), jnp.bfloat16),
            pltpu.SemaphoreType.DMA((6,)),
        ],
        compiler_params=params,
        name="model",
    )(
        away(positions[0, 0]), away(mode_weights[0, 0]), own, above, below, from_left, from_right,
        away(probe_mean), away(probe_basis), away(amplitudes[0, 0]),
        away(jnp.asarray(tables(n))),
    )

    cores = 2
    per_core = count_x // cores
    columns = [[cores * at + core for at in range(per_core)] for core in range(cores)]
    layers = [
        [row * count_x + cores * at + core for row in range(count_y) for core in range(cores)]
        for at in range(per_core)
    ]
    gathered = exchange(probe_grad, ("sy", "sx"), layers)
    from_left = lax.ppermute(to_right, "sx", forward_x)
    from_right = lax.ppermute(to_left, "sx", backward_x)
    gathered, from_left, from_right = lax.optimization_barrier((gathered, from_left, from_right))
    parts = pl.pallas_call(
        mix_kernel,
        out_shape=jax.ShapeDtypeStruct((per_core, modes // 2, 8, n), f32),
        in_specs=vmem_specs(1),
        out_specs=vmem_specs(1)[0],
        scratch_shapes=[pltpu.VMEM((4 * modes, n), f32)],
        compiler_params=params,
        name="mix",
    )(gathered)
    parts = exchange(parts, "sx", columns)
    up, middle, down = pl.pallas_call(
        merge_kernel,
        out_shape=(edge, block, edge),
        in_specs=vmem_specs(3),
        out_specs=tuple(vmem_specs(3)),
        compiler_params=params,
        name="merge",
    )(tall, from_left, from_right)
    from_below = lax.ppermute(up, "sy", backward_y)
    from_above = lax.ppermute(down, "sy", forward_y)
    parts, from_below, from_above = lax.optimization_barrier((parts, from_below, from_above))
    parts = pl.pallas_call(
        repeat_kernel,
        out_shape=jax.ShapeDtypeStruct((count_y,) + parts.shape[1:], f32),
        in_specs=vmem_specs(1),
        out_specs=vmem_specs(1)[0],
        compiler_params=params,
        name="repeat",
    )(parts)
    mine = exchange(parts, "sy")
    swap = [(at, at ^ 1) for at in range(count_x)]
    other = lax.ppermute(mine, "sx", swap)
    core = (lax.axis_index("sx") % cores).astype(jnp.int32).reshape(1)
    count_all = per_tile * count_y * count_x
    step_len = 1.0 / math.sqrt(count_all)

    def final_kernel(*refs):
        ortho_kernel(*refs, step_len=step_len)

    new_basis = pl.pallas_call(
        final_kernel,
        out_shape=jax.ShapeDtypeStruct((modes, 2 * blocks, 8, n), f32),
        in_specs=[smem] + vmem_specs(3),
        out_specs=vmem_specs(1)[0],
        compiler_params=params,
        name="orthonormal",
    )(core, mine, other, probe_basis.reshape(modes, 2 * blocks, 8, n))
    new_basis = new_basis.reshape(probe_basis.shape)

    obj_grad = middle + jnp.concatenate([from_above, from_below], axis=1)
    return (obj_grad.reshape(obj_delta.shape), new_basis)


def solution(mesh):
    placed = (
        P(None, None, "sy", "sx"),
        P(),
        P(),
        P("sy", "sx", None, None),
        P("sy", "sx", None, None),
        P("sy", "sx", None, None, None),
    )
    return jax.shard_map(
        local,
        mesh=mesh,
        in_specs=placed,
        out_specs=(P(None, None, "sy", "sx"), P()),
        check_vma=False,
    )
```

```python
import math

import jax
import jax.numpy as jnp
import numpy as np
from jax import lax
from jax.experimental import pallas as pl
from jax.experimental.pallas import tpu as pltpu
from jax.sharding import PartitionSpec as P

FLOOR = 0.5
PHASE_EDGE = 3.0
VMEM_BYTES = 40 * 1024 * 1024
PIECE = 9


def split_table(values):
    whole = values.astype(np.float32)
    high = whole.astype(jnp.bfloat16)
    low = (whole - high.astype(np.float32)).astype(jnp.bfloat16)
    return np.stack([high, low])


def tables(probe_len):
    indices = np.arange(probe_len)
    dft = np.exp(-2j * np.pi * (np.outer(indices, indices) % probe_len) / probe_len)
    dft = dft / math.sqrt(probe_len)
    half = probe_len // 2
    frequency = ((indices + half) % probe_len - half) / half
    phase = np.exp(-1j * PHASE_EDGE * frequency * frequency)
    move = np.conj(dft) @ (phase[:, None] * dft)
    parts = [split_table(part) for form in (dft, move) for part in (form.real, form.imag)]
    return np.stack(parts)


def block_forms(real, imag):
    above = jnp.concatenate([real, -imag], axis=1)
    below = jnp.concatenate([imag, real], axis=1)
    above_t = jnp.concatenate([real, imag], axis=1)
    below_t = jnp.concatenate([-imag, real], axis=1)
    return (
        jnp.concatenate([above, below], axis=0),
        jnp.concatenate([above_t, below_t], axis=0),
    )


def dot3(left, right):
    left_high, left_low = left
    right_high, right_low = right
    return jnp.dot(
        jnp.concatenate([left_high, left_low, left_high], axis=1),
        jnp.concatenate([right_low, right_high, right_high], axis=0),
        preferred_element_type=jnp.float32,
    )


def halves(values):
    high = values.astype(jnp.bfloat16)
    low = (values - high.astype(jnp.float32)).astype(jnp.bfloat16)
    return (high, low)


def both_sides(fields, left_table, right_table):
    (real0, imag0), (real1, imag1) = fields
    n = real0.shape[0]
    upright = jnp.concatenate(
        [jnp.concatenate([real0, real1], axis=1), jnp.concatenate([imag0, imag1], axis=1)], axis=0
    )
    upright = dot3(left_table, halves(upright))
    top, bottom = upright[:n], upright[n:]
    wide = jnp.concatenate(
        [
            jnp.concatenate([top[:, :n], bottom[:, :n]], axis=1),
            jnp.concatenate([top[:, n:], bottom[:, n:]], axis=1),
        ],
        axis=0,
    )
    wide = dot3(halves(wide), right_table)
    return [(wide[:n, :n], wide[:n, n:]), (wide[n:, :n], wide[n:, n:])]


def near_lanes(shape):
    return lax.broadcasted_iota(jnp.int32, shape, len(shape) - 1) < shape[-1] // 2


def roll_planes(values):
    return jnp.stack([pltpu.roll(plane, plane.shape[-1] // 2, 1) for plane in values])


def split_kernel(source, own, upper, lower, sems):
    half = upper.shape[1]
    copies = [
        pltpu.make_async_copy(source.at[:, 0:half], upper, sems.at[0]),
        pltpu.make_async_copy(source.at[:, half : 2 * half], lower, sems.at[1]),
        pltpu.make_async_copy(source, own, sems.at[2]),
    ]
    for copy in copies:
        copy.start()
    for copy in copies:
        copy.wait()


def repeat_kernel(parts, out):
    total = parts[0]
    for at in range(1, parts.shape[0]):
        total = total + parts[at]
    for at in range(out.shape[0]):
        out[at] = total


def pack_kernel(own, above, below, to_left, to_right):
    n = own.shape[-1]
    half = n // 2
    near = near_lanes(own.shape)
    first = jnp.concatenate([above[...], own[:, :half]], axis=1)
    second = jnp.concatenate([own[:, half:], below[...]], axis=1)
    second = roll_planes(second)
    to_left[...] = jnp.where(near, first, second)
    to_right[...] = jnp.where(near, second, first)


def merge_kernel(wide, from_above, from_below, middle, to_left, to_right):
    n = middle.shape[-1]
    half = n // 2
    upper = wide[:, :half] + from_above[...]
    lower = wide[:, half:] + from_below[...]
    middle[:, :half] = upper[:, :, :n]
    middle[:, half:] = lower[:, :, :n]
    first = upper[:, :, n:]
    second = roll_planes(lower[:, :, n:])
    near = near_lanes(first.shape)
    to_right[...] = jnp.where(near, first, second)
    to_left[...] = jnp.where(near, second, first)


def finish_kernel(middle, from_left, from_right, out):
    half = middle.shape[1] // 2
    near = near_lanes(from_left.shape)
    left, right = from_left[...], from_right[...]
    out[:, :half] = middle[:, :half] + jnp.where(near, left, right)
    out[:, half:] = middle[:, half:] + roll_planes(jnp.where(near, right, left))


def prepare_kernel(
    after, weights_in, mean_in, basis_in, measured_in, table_in,
    probes, forms, measured, packed, weights, mean, basis, table, sems,
):
    del after
    copies = [
        pltpu.make_async_copy(source, target, sems.at[at])
        for at, (source, target) in enumerate(
            [
                (weights_in, weights),
                (table_in, table),
                (mean_in, mean),
                (basis_in, basis),
                (measured_in, measured),
            ]
        )
    ]
    for copy in copies:
        copy.start()
    n = mean.shape[-1]
    modes = basis.shape[0]
    slots = range(2)
    copies[0].wait()
    lane_at = lax.broadcasted_iota(jnp.int32, (1, n), 1)
    row = jnp.zeros((1, n), jnp.float32)
    for slot in slots:
        for mode in range(modes):
            row = jnp.where(lane_at == slot * modes + mode, weights[slot, mode], row)
    packed[...] = row
    copies[1].wait()
    for at in range(2):
        for part in range(2):
            form, form_t = block_forms(table[2 * at, part], table[2 * at + 1, part])
            forms[2 * at, part] = form
            forms[2 * at + 1, part] = form_t
    copies[2].wait()
    copies[3].wait()
    for slot in slots:
        real = mean[0]
        imag = mean[1]
        for mode in range(modes):
            real = real + weights[slot, mode] * basis[mode, 0]
            imag = imag + weights[slot, mode] * basis[mode, 1]
        probes[slot, 0] = real
        probes[slot, 1] = imag
    copies[4].wait()


def model_kernel(
    positions_in, own, above, below, from_left, from_right, probes_in, forms, measured, packed,
    probe_grad, terms, frame, positions, sem,
):
    copy = pltpu.make_async_copy(positions_in, positions, sem)
    copy.start()
    n = measured.shape[-1]
    half = n // 2
    near = near_lanes(own.shape)
    frame[:, 0:half, 0:n] = above[...]
    frame[:, half : half + n, 0:n] = own[...]
    frame[:, half + n : 2 * n, 0:n] = below[...]
    frame[:, 0:n, n : 2 * n] = jnp.where(near, from_right[...], from_left[...])
    frame[:, n : 2 * n, n : 2 * n] = roll_planes(
        jnp.where(near, from_left[...], from_right[...])
    )
    slots = range(2)
    copy.wait()
    rows = [positions[slot, 0] for slot in slots]
    cols = [positions[slot, 1] for slot in slots]
    offsets = [row & 7 for row in rows]
    bases = [pl.multiple_of(row - offset, 8) for row, offset in zip(rows, offsets)]
    span = n + 8

    def window(slot, plane):
        strip = frame[plane, pl.ds(bases[slot], span), :]
        strip = pltpu.roll(strip, (5 * half - cols[slot]) & (2 * n - 1), 1)[:, :n]
        shift = jnp.where(offsets[slot] == 0, 0, span - offsets[slot])
        return pltpu.roll(strip, shift, 0)[:n]

    transmit = [
        [(1.0 + window(slot, 2 * layer), window(slot, 2 * layer + 1)) for slot in slots]
        for layer in range(2)
    ]
    probes = [(probes_in[slot, 0], probes_in[slot, 1]) for slot in slots]
    dft, dft_t, move, move_t = [(forms[at, 0], forms[at, 1]) for at in range(4)]

    def times(first, second):
        return [(a * c - b * d, a * d + b * c) for (a, b), (c, d) in zip(first, second)]

    def conj_times(first, second):
        return [(a * c + b * d, a * d - b * c) for (a, b), (c, d) in zip(first, second)]

    def keep(layer, pairs):
        for slot in slots:
            for part in range(2):
                terms[layer, slot, part] = pairs[slot][part]

    entered = both_sides(times(probes, transmit[0]), move, move_t)
    far = both_sides(times(entered, transmit[1]), dft, dft_t)
    chi = []
    for slot in slots:
        real, imag = far[slot]
        modulus = jnp.maximum(jnp.sqrt(real * real + imag * imag), FLOOR)
        ratio = measured[slot] / modulus
        chi.append((real - real * ratio, imag - imag * ratio))
    back = both_sides(chi, dft_t, dft)
    keep(1, conj_times(entered, back))
    back = both_sides(conj_times(transmit[1], back), move_t, move)
    keep(0, conj_times(probes, back))
    back = conj_times(transmit[0], back)
    blocks = n // 8
    upper_rows = lax.broadcasted_iota(jnp.int32, (8, n), 0) < 4
    for part in range(2):
        for block in range(blocks):
            first = back[0][part][8 * block : 8 * block + 8]
            second = back[1][part][8 * block : 8 * block + 8]
            at = 2 * PIECE * (part * blocks + block)
            probe_grad[pl.ds(at, 8), 0, :] = jnp.where(
                upper_rows, first, pltpu.roll(second, 4, 0)
            )
            probe_grad[at + 8] = packed[...]
            probe_grad[pl.ds(at + PIECE, 8), 0, :] = jnp.where(
                upper_rows, pltpu.roll(first, 4, 0), second
            )
            probe_grad[at + PIECE + 8] = packed[...]


def deposit_kernel(positions_in, terms, up, wide, down, grads, positions, sem):
    copy = pltpu.make_async_copy(positions_in, positions, sem)
    copy.start()
    n = terms.shape[-1]
    half = n // 2
    span = n + 8
    grads[...] = jnp.zeros(grads.shape, jnp.float32)
    copy.wait()
    for slot in range(2):
        row, col = positions[slot, 0], positions[slot, 1]
        offset = row & 7
        base = pl.multiple_of(row - offset, 8)
        for plane in range(4):
            padded = jnp.concatenate(
                [terms[plane // 2, slot, plane % 2], jnp.zeros((8, n), jnp.float32)], axis=0
            )
            lowered = pltpu.roll(padded, offset, 0)
            padded = jnp.concatenate([lowered, jnp.zeros((span, n), jnp.float32)], axis=1)
            shifted = pltpu.roll(padded, (col + 3 * half) & (2 * n - 1), 1)
            at = (plane, pl.ds(base, span), slice(None))
            grads[at] = grads[at] + shifted
    up[...] = grads[:, 0:half]
    wide[...] = grads[:, half : half + n]
    down[...] = grads[:, half + n : 2 * n]


def mix_kernel(gathered, out, ordered):
    copies, pairs, rows, n = out.shape
    modes = 2 * pairs
    some = rows // 2
    count = gathered.shape[0] // PIECE

    def row_of_all(at):
        return gathered[pl.ds(at, count, stride=PIECE), 0, :]

    factors = row_of_all(rows).T[: 2 * modes]
    terms = jnp.concatenate([row_of_all(at) for at in range(rows)], axis=1)
    product = jnp.dot(
        factors, terms, precision=lax.Precision.HIGHEST, preferred_element_type=jnp.float32
    )
    for row in range(some):
        first = product[:modes, row * n : (row + 1) * n]
        second = product[modes:, (some + row) * n : (some + row + 1) * n]
        ordered[pl.ds(row, modes, stride=some), :] = first + second
    for pair in range(pairs):
        tile = ordered[pair * rows : (pair + 1) * rows]
        for copy in range(copies):
            out[copy, pair] = tile


def ortho_kernel(core, mine, other, basis, out, step_len=None):
    modes, blocks, rows, n = out.shape
    part_len = blocks // 2
    pixels = part_len * rows * n
    upper_rows = lax.broadcasted_iota(jnp.int32, (rows, n), 0) < rows // 2
    first_core = core[0] == 0
    for block in range(blocks):
        for pair in range(modes // 2):
            low = jnp.where(first_core, mine[block, pair], other[block, pair])
            high = jnp.where(first_core, other[block, pair], mine[block, pair])
            even = jnp.where(upper_rows, low, pltpu.roll(high, rows // 2, 0))
            odd = jnp.where(upper_rows, pltpu.roll(low, rows // 2, 0), high)
            out[2 * pair, block] = basis[2 * pair, block] - step_len * even
            out[2 * pair + 1, block] = basis[2 * pair + 1, block] - step_len * odd

    def total(values):
        return jnp.sum(jnp.sum(values, axis=0), axis=(0, 1), keepdims=True)

    for mode in range(modes):
        real = out[mode, 0:part_len]
        imag = out[mode, part_len:blocks]
        norm = total(real * real + imag * imag)
        for later in range(mode + 1, modes):
            later_real = out[later, 0:part_len]
            later_imag = out[later, part_len:blocks]
            factor_real = (total(real * later_real + imag * later_imag) / norm)[None]
            factor_imag = (total(real * later_imag - imag * later_real) / norm)[None]
            out[later, 0:part_len] = later_real - (factor_real * real - factor_imag * imag)
            out[later, part_len:blocks] = later_imag - (factor_real * imag + factor_imag * real)
        scale = (1.0 / jnp.sqrt(norm / pixels))[None]
        out[mode, 0:part_len] = real * scale
        out[mode, part_len:blocks] = imag * scale


def shift_pairs(count):
    forward = [(at, at + 1) for at in range(count - 1)]
    return forward, [(target, source) for source, target in forward]


def exchange(values, axis, groups=None):
    return lax.all_to_all(values, axis, 0, 0, tiled=True, axis_index_groups=groups)


def away(values):
    return pltpu.with_memory_space_constraint(values, pltpu.HBM)


def vmem_specs(count):
    return [pl.BlockSpec(memory_space=pltpu.VMEM)] * count


def local(obj_delta, probe_mean, probe_basis, mode_weights, positions, amplitudes):
    n = probe_mean.shape[-1]
    half = n // 2
    modes = probe_basis.shape[0]
    per_tile = positions.shape[2]
    count_y, count_x = lax.axis_size("sy"), lax.axis_size("sx")
    forward_y, backward_y = shift_pairs(count_y)
    forward_x, backward_x = shift_pairs(count_x)
    planes = obj_delta.shape[0] * obj_delta.shape[1]
    blocks = n // 8
    params = pltpu.CompilerParams(vmem_limit_bytes=VMEM_BYTES)
    smem = pl.BlockSpec(memory_space=pltpu.SMEM)

    f32 = jnp.float32
    block = jax.ShapeDtypeStruct((planes, n, n), f32)
    edge = jax.ShapeDtypeStruct((planes, half, n), f32)
    distant = pl.BlockSpec(memory_space=pltpu.HBM)
    own, upper, lower = pl.pallas_call(
        split_kernel,
        out_shape=(block, edge, edge),
        in_specs=[distant],
        out_specs=tuple(vmem_specs(3)),
        scratch_shapes=[pltpu.SemaphoreType.DMA((3,))],
        compiler_params=params,
        name="split",
    )(away(obj_delta.reshape(planes, n, n)))
    above = lax.ppermute(lower, "sy", forward_y)
    below = lax.ppermute(upper, "sy", backward_y)
    bf16 = jnp.bfloat16
    probes, forms, measured, packed = pl.pallas_call(
        prepare_kernel,
        out_shape=(
            jax.ShapeDtypeStruct((per_tile, 2, n, n), f32),
            jax.ShapeDtypeStruct((4, 2, 2 * n, 2 * n), bf16),
            jax.ShapeDtypeStruct((per_tile, n, n), f32),
            jax.ShapeDtypeStruct((1, n), f32),
        ),
        in_specs=vmem_specs(1) + [distant] * 5,
        out_specs=tuple(vmem_specs(4)),
        scratch_shapes=[
            pltpu.SMEM((per_tile, modes), f32),
            pltpu.VMEM((2, n, n), f32),
            pltpu.VMEM((modes, 2, n, n), f32),
            pltpu.VMEM((4, 2, n, n), bf16),
            pltpu.SemaphoreType.DMA((5,)),
        ],
        compiler_params=params,
        name="prepare",
    )(
        upper, away(mode_weights[0, 0]), away(probe_mean), away(probe_basis),
        away(amplitudes[0, 0]), away(jnp.asarray(tables(n))),
    )
    above, below, probes, forms, measured, packed = lax.optimization_barrier(
        (above, below, probes, forms, measured, packed)
    )
    to_left, to_right = pl.pallas_call(
        pack_kernel,
        out_shape=(block, block),
        in_specs=vmem_specs(3),
        out_specs=tuple(vmem_specs(2)),
        compiler_params=params,
        name="pack",
    )(own, above, below)
    from_left = lax.ppermute(to_right, "sx", forward_x)
    from_right = lax.ppermute(to_left, "sx", backward_x)

    probe_grad, terms = pl.pallas_call(
        model_kernel,
        out_shape=(
            jax.ShapeDtypeStruct((4 * blocks * PIECE, 1, n), f32),
            jax.ShapeDtypeStruct((2, per_tile, 2, n, n), f32),
        ),
        in_specs=[distant] + vmem_specs(9),
        out_specs=tuple(vmem_specs(2)),
        scratch_shapes=[
            pltpu.VMEM((planes, 2 * n, 2 * n), f32),
            pltpu.SMEM((per_tile, 2), jnp.int32),
            pltpu.SemaphoreType.DMA(()),
        ],
        compiler_params=params,
        name="model",
    )(
        away(positions[0, 0]), own, above, below, from_left, from_right,
        probes, forms, measured, packed,
    )
    wide_edge = jax.ShapeDtypeStruct((planes, half, 2 * n), f32)
    up, wide, down = pl.pallas_call(
        deposit_kernel,
        out_shape=(wide_edge, jax.ShapeDtypeStruct((planes, n, 2 * n), f32), wide_edge),
        in_specs=[distant] + vmem_specs(1),
        out_specs=tuple(vmem_specs(3)),
        scratch_shapes=[
            pltpu.VMEM((planes, 2 * n, 2 * n), f32),
            pltpu.SMEM((per_tile, 2), jnp.int32),
            pltpu.SemaphoreType.DMA(()),
        ],
        compiler_params=params,
        name="deposit",
    )(away(positions[0, 0]), terms)

    cores = 2
    per_core = count_x // cores
    columns = [[cores * at + core for at in range(per_core)] for core in range(cores)]
    layers = [
        [row * count_x + cores * at + core for row in range(count_y) for core in range(cores)]
        for at in range(per_core)
    ]
    gathered = exchange(probe_grad, ("sy", "sx"), layers)
    parts = pl.pallas_call(
        mix_kernel,
        out_shape=jax.ShapeDtypeStruct((per_core, modes // 2, 8, n), f32),
        in_specs=vmem_specs(1),
        out_specs=vmem_specs(1)[0],
        scratch_shapes=[pltpu.VMEM((4 * modes, n), f32)],
        compiler_params=params,
        name="mix",
    )(gathered)
    parts = exchange(parts, "sx", columns)
    from_below = lax.ppermute(up, "sy", backward_y)
    from_above = lax.ppermute(down, "sy", forward_y)
    parts, from_below, from_above = lax.optimization_barrier((parts, from_below, from_above))
    middle, to_left, to_right = pl.pallas_call(
        merge_kernel,
        out_shape=(block, edge, edge),
        in_specs=vmem_specs(3),
        out_specs=tuple(vmem_specs(3)),
        compiler_params=params,
        name="merge",
    )(wide, from_above, from_below)
    parts = pl.pallas_call(
        repeat_kernel,
        out_shape=jax.ShapeDtypeStruct((count_y,) + parts.shape[1:], f32),
        in_specs=vmem_specs(1),
        out_specs=vmem_specs(1)[0],
        compiler_params=params,
        name="repeat",
    )(parts)
    mine = exchange(parts, "sy")
    from_left = lax.ppermute(to_right, "sx", forward_x)
    from_right = lax.ppermute(to_left, "sx", backward_x)
    obj_grad = pl.pallas_call(
        finish_kernel,
        out_shape=block,
        in_specs=vmem_specs(3),
        out_specs=vmem_specs(1)[0],
        compiler_params=params,
        name="finish",
    )(middle, from_left, from_right)
    mine, obj_grad = lax.optimization_barrier((mine, obj_grad))
    swap = [(at, at ^ 1) for at in range(count_x)]
    other = lax.ppermute(mine, "sx", swap)
    core = (lax.axis_index("sx") % cores).astype(jnp.int32).reshape(1)
    count_all = per_tile * count_y * count_x
    step_len = 1.0 / math.sqrt(count_all)

    def final_kernel(*refs):
        ortho_kernel(*refs, step_len=step_len)

    new_basis = pl.pallas_call(
        final_kernel,
        out_shape=jax.ShapeDtypeStruct((modes, 2 * blocks, 8, n), f32),
        in_specs=[smem] + vmem_specs(3),
        out_specs=vmem_specs(1)[0],
        compiler_params=params,
        name="orthonormal",
    )(core, mine, other, probe_basis.reshape(modes, 2 * blocks, 8, n))
    new_basis = new_basis.reshape(probe_basis.shape)

    return (obj_grad.reshape(obj_delta.shape), new_basis)


def solution(mesh):
    placed = (
        P(None, None, "sy", "sx"),
        P(),
        P(),
        P("sy", "sx", None, None),
        P("sy", "sx", None, None),
        P("sy", "sx", None, None, None),
    )
    return jax.shard_map(
        local,
        mesh=mesh,
        in_specs=placed,
        out_specs=(P(None, None, "sy", "sx"), P()),
        check_vma=False,
    )
```

```python
import functools
import math

import jax
import jax.numpy as jnp
import numpy as np
from jax import lax
from jax.experimental import pallas as pl
from jax.experimental.pallas import tpu as pltpu
from jax.sharding import PartitionSpec as P

FLOOR = 0.5
PHASE_EDGE = 3.0
VMEM_BYTES = 40 * 1024 * 1024
PIECE = 9


def split_table(values):
    whole = values.astype(np.float32)
    high = whole.astype(jnp.bfloat16)
    low = (whole - high.astype(np.float32)).astype(jnp.bfloat16)
    return np.stack([high, low])


def tables(probe_len):
    indices = np.arange(probe_len)
    dft = np.exp(-2j * np.pi * (np.outer(indices, indices) % probe_len) / probe_len)
    dft = dft / math.sqrt(probe_len)
    half = probe_len // 2
    frequency = ((indices + half) % probe_len - half) / half
    phase = np.exp(-1j * PHASE_EDGE * frequency * frequency)
    move = np.conj(dft) @ (phase[:, None] * dft)
    parts = [split_table(part) for form in (dft, move) for part in (form.real, form.imag)]
    return np.stack(parts)


def block_forms(real, imag):
    above = jnp.concatenate([real, -imag], axis=1)
    below = jnp.concatenate([imag, real], axis=1)
    above_t = jnp.concatenate([real, imag], axis=1)
    below_t = jnp.concatenate([-imag, real], axis=1)
    return (
        jnp.concatenate([above, below], axis=0),
        jnp.concatenate([above_t, below_t], axis=0),
    )


def dot3(left, right):
    left_high, left_low = left
    right_high, right_low = right
    return jnp.dot(
        jnp.concatenate([left_high, left_low, left_high], axis=1),
        jnp.concatenate([right_low, right_high, right_high], axis=0),
        preferred_element_type=jnp.float32,
    )


def halves(values):
    high = values.astype(jnp.bfloat16)
    low = (values - high.astype(jnp.float32)).astype(jnp.bfloat16)
    return (high, low)


def both_sides(fields, left_table, right_table):
    (real0, imag0), (real1, imag1) = fields
    n = real0.shape[0]
    upright = jnp.concatenate(
        [jnp.concatenate([real0, real1], axis=1), jnp.concatenate([imag0, imag1], axis=1)], axis=0
    )
    upright = dot3(left_table, halves(upright))
    top, bottom = upright[:n], upright[n:]
    wide = jnp.concatenate(
        [
            jnp.concatenate([top[:, :n], bottom[:, :n]], axis=1),
            jnp.concatenate([top[:, n:], bottom[:, n:]], axis=1),
        ],
        axis=0,
    )
    wide = dot3(halves(wide), right_table)
    return [(wide[:n, :n], wide[:n, n:]), (wide[n:, :n], wide[n:, n:])]


def near_lanes(shape):
    return lax.broadcasted_iota(jnp.int32, shape, len(shape) - 1) < shape[-1] // 2


def roll_planes(values):
    return jnp.stack([pltpu.roll(plane, plane.shape[-1] // 2, 1) for plane in values])


def split_kernel(source, upper, lower, sems):
    half = upper.shape[1]
    copies = [
        pltpu.make_async_copy(source.at[:, 0:half], upper, sems.at[0]),
        pltpu.make_async_copy(source.at[:, half : 2 * half], lower, sems.at[1]),
    ]
    for copy in copies:
        copy.start()
    for copy in copies:
        copy.wait()


def repeat_kernel(parts, out):
    total = parts[0]
    for at in range(1, parts.shape[0]):
        total = total + parts[at]
    for at in range(out.shape[0]):
        out[at] = total


def pack_kernel(upper, lower, above, below, to_left, to_right):
    near = near_lanes(to_left.shape)
    first = jnp.concatenate([above[...], upper[...]], axis=1)
    second = jnp.concatenate([lower[...], below[...]], axis=1)
    second = roll_planes(second)
    to_left[...] = jnp.where(near, first, second)
    to_right[...] = jnp.where(near, second, first)


def merge_kernel(wide, from_above, from_below, middle, to_left, to_right):
    n = middle.shape[-1]
    half = n // 2
    upper = wide[:, :half] + from_above[...]
    lower = wide[:, half:] + from_below[...]
    middle[:, :half] = upper[:, :, :n]
    middle[:, half:] = lower[:, :, :n]
    first = upper[:, :, n:]
    second = roll_planes(lower[:, :, n:])
    near = near_lanes(first.shape)
    to_right[...] = jnp.where(near, first, second)
    to_left[...] = jnp.where(near, second, first)


def finish_kernel(middle, from_left, from_right, out):
    half = middle.shape[1] // 2
    near = near_lanes(from_left.shape)
    left, right = from_left[...], from_right[...]
    out[:, :half] = middle[:, :half] + jnp.where(near, left, right)
    out[:, half:] = middle[:, half:] + roll_planes(jnp.where(near, right, left))


def prepare_kernel(
    after, weights_in, mean_in, basis_in, measured_in, table_in,
    probes, forms, measured, packed, weights, mean, basis, table, sems,
):
    del after
    copies = [
        pltpu.make_async_copy(source, target, sems.at[at])
        for at, (source, target) in enumerate(
            [
                (weights_in, weights),
                (table_in, table),
                (mean_in, mean),
                (basis_in, basis),
                (measured_in, measured),
            ]
        )
    ]
    for copy in copies:
        copy.start()
    n = mean.shape[-1]
    modes = basis.shape[0]
    slots = range(2)
    copies[0].wait()
    lane_at = lax.broadcasted_iota(jnp.int32, (1, n), 1)
    row = jnp.zeros((1, n), jnp.float32)
    for slot in slots:
        for mode in range(modes):
            row = jnp.where(lane_at == slot * modes + mode, weights[slot, mode], row)
    packed[...] = row
    copies[1].wait()
    for at in range(2):
        for part in range(2):
            form, form_t = block_forms(table[2 * at, part], table[2 * at + 1, part])
            forms[2 * at, part] = form
            forms[2 * at + 1, part] = form_t
    copies[2].wait()
    copies[3].wait()
    for slot in slots:
        real = mean[0]
        imag = mean[1]
        for mode in range(modes):
            real = real + weights[slot, mode] * basis[mode, 0]
            imag = imag + weights[slot, mode] * basis[mode, 1]
        probes[slot, 0] = real
        probes[slot, 1] = imag
    copies[4].wait()


def model_kernel(
    positions_in, upper, lower, above, below, from_left, from_right, probes_in, forms, measured, packed,
    probe_grad, terms, frame, positions, sem,
):
    copy = pltpu.make_async_copy(positions_in, positions, sem)
    copy.start()
    n = measured.shape[-1]
    half = n // 2
    near = near_lanes(from_left.shape)
    frame[:, 0:half, 0:n] = above[...]
    frame[:, half:n, 0:n] = upper[...]
    frame[:, n : n + half, 0:n] = lower[...]
    frame[:, half + n : 2 * n, 0:n] = below[...]
    frame[:, 0:n, n : 2 * n] = jnp.where(near, from_right[...], from_left[...])
    frame[:, n : 2 * n, n : 2 * n] = roll_planes(
        jnp.where(near, from_left[...], from_right[...])
    )
    slots = range(2)
    copy.wait()
    rows = [positions[slot, 0] for slot in slots]
    cols = [positions[slot, 1] for slot in slots]
    offsets = [row & 7 for row in rows]
    bases = [pl.multiple_of(row - offset, 8) for row, offset in zip(rows, offsets)]
    span = n + 8

    def window(slot, plane):
        strip = frame[plane, pl.ds(bases[slot], span), :]
        strip = pltpu.roll(strip, (5 * half - cols[slot]) & (2 * n - 1), 1)[:, :n]
        shift = jnp.where(offsets[slot] == 0, 0, span - offsets[slot])
        return pltpu.roll(strip, shift, 0)[:n]

    transmit = [
        [(1.0 + window(slot, 2 * layer), window(slot, 2 * layer + 1)) for slot in slots]
        for layer in range(2)
    ]
    probes = [(probes_in[slot, 0], probes_in[slot, 1]) for slot in slots]
    dft, dft_t, move, move_t = [(forms[at, 0], forms[at, 1]) for at in range(4)]

    def times(first, second):
        return [(a * c - b * d, a * d + b * c) for (a, b), (c, d) in zip(first, second)]

    def conj_times(first, second):
        return [(a * c + b * d, a * d - b * c) for (a, b), (c, d) in zip(first, second)]

    def keep(layer, pairs):
        for slot in slots:
            for part in range(2):
                terms[layer, slot, part] = pairs[slot][part]

    entered = both_sides(times(probes, transmit[0]), move, move_t)
    far = both_sides(times(entered, transmit[1]), dft, dft_t)
    chi = []
    for slot in slots:
        real, imag = far[slot]
        modulus = jnp.maximum(jnp.sqrt(real * real + imag * imag), FLOOR)
        ratio = measured[slot] / modulus
        chi.append((real - real * ratio, imag - imag * ratio))
    back = both_sides(chi, dft_t, dft)
    keep(1, conj_times(entered, back))
    back = both_sides(conj_times(transmit[1], back), move_t, move)
    keep(0, conj_times(probes, back))
    back = conj_times(transmit[0], back)
    blocks = n // 8
    upper_rows = lax.broadcasted_iota(jnp.int32, (8, n), 0) < 4
    for part in range(2):
        for block in range(blocks):
            first = back[0][part][8 * block : 8 * block + 8]
            second = back[1][part][8 * block : 8 * block + 8]
            at = 2 * PIECE * (part * blocks + block)
            probe_grad[pl.ds(at, 8), 0, :] = jnp.where(
                upper_rows, first, pltpu.roll(second, 4, 0)
            )
            probe_grad[at + 8] = packed[...]
            probe_grad[pl.ds(at + PIECE, 8), 0, :] = jnp.where(
                upper_rows, pltpu.roll(first, 4, 0), second
            )
            probe_grad[at + PIECE + 8] = packed[...]


def deposit_kernel(positions_in, terms, up, wide, down, grads, positions, sem):
    copy = pltpu.make_async_copy(positions_in, positions, sem)
    copy.start()
    n = terms.shape[-1]
    half = n // 2
    span = n + 8
    grads[...] = jnp.zeros(grads.shape, jnp.float32)
    copy.wait()
    for slot in range(2):
        row, col = positions[slot, 0], positions[slot, 1]
        offset = row & 7
        base = pl.multiple_of(row - offset, 8)
        for plane in range(4):
            padded = jnp.concatenate(
                [terms[plane // 2, slot, plane % 2], jnp.zeros((8, n), jnp.float32)], axis=0
            )
            lowered = pltpu.roll(padded, offset, 0)
            padded = jnp.concatenate([lowered, jnp.zeros((span, n), jnp.float32)], axis=1)
            shifted = pltpu.roll(padded, (col + 3 * half) & (2 * n - 1), 1)
            at = (plane, pl.ds(base, span), slice(None))
            grads[at] = grads[at] + shifted
    up[...] = grads[:, 0:half]
    wide[...] = grads[:, half : half + n]
    down[...] = grads[:, half + n : 2 * n]


def mix_kernel(gathered, out, ordered):
    copies, pairs, rows, n = out.shape
    modes = 2 * pairs
    some = rows // 2
    count = gathered.shape[0] // PIECE

    def row_of_all(at):
        return gathered[pl.ds(at, count, stride=PIECE), 0, :]

    factors = row_of_all(rows).T[: 2 * modes]
    terms = jnp.concatenate([row_of_all(at) for at in range(rows)], axis=1)
    product = jnp.dot(
        factors, terms, precision=lax.Precision.HIGHEST, preferred_element_type=jnp.float32
    )
    for row in range(some):
        first = product[:modes, row * n : (row + 1) * n]
        second = product[modes:, (some + row) * n : (some + row + 1) * n]
        ordered[pl.ds(row, modes, stride=some), :] = first + second
    for pair in range(pairs):
        tile = ordered[pair * rows : (pair + 1) * rows]
        for copy in range(copies):
            out[copy, pair] = tile


def products(pairs, sums):
    tiles, blocks, rows = pairs.shape[0], pairs.shape[1], pairs.shape[2]
    parts = blocks // 2
    sums = list(sums)
    for block in range(parts):
        real = [pairs[at, block] for at in range(tiles)]
        imag = [pairs[at, parts + block] for at in range(tiles)]
        turned_real = [pltpu.roll(values, rows // 2, 0) for values in real]
        turned_imag = [pltpu.roll(values, rows // 2, 0) for values in imag]
        at = 0
        for first in range(tiles):
            a, b = real[first], imag[first]
            for second in range(first, tiles):
                c, d = real[second], imag[second]
                sums[at] = sums[at] + (a * c + b * d)
                at += 1
                if second > first:
                    sums[at] = sums[at] + (a * d - b * c)
                    at += 1
                c, d = turned_real[second], turned_imag[second]
                sums[at] = sums[at] + (a * c + b * d)
                sums[at + 1] = sums[at + 1] + (a * d - b * c)
                at += 2
    return sums


def own_kernel(core, mine, basis, own_pairs, base_pairs, sums_out, step_len=None):
    tiles, blocks, rows, n = own_pairs.shape
    upper_rows = lax.broadcasted_iota(jnp.int32, (rows, n), 0) < rows // 2
    first_core = core[0] == 0
    for block in range(blocks):
        for at in range(tiles):
            even, odd = basis[2 * at, block], basis[2 * at + 1, block]
            low = jnp.where(upper_rows, even, pltpu.roll(odd, rows // 2, 0))
            high = jnp.where(upper_rows, pltpu.roll(even, rows // 2, 0), odd)
            base = jnp.where(first_core, low, high)
            own_pairs[at, block] = base - step_len * mine[block, at]
            base_pairs[at, block] = jnp.where(first_core, high, low)
    zero = jnp.zeros((rows, n), jnp.float32)
    sums = products(own_pairs, [zero] * sums_out.shape[0])
    for at, values in enumerate(sums):
        sums_out[at] = values


def ortho_kernel(
    core, other, own_pairs, base_pairs, sums_in, out, other_pairs, result, sems, step_len=None
):
    tiles, blocks, rows, n = own_pairs.shape
    modes = 2 * tiles
    parts = blocks // 2
    pixels = parts * rows * n
    half = rows // 2
    upper_rows = lax.broadcasted_iota(jnp.int32, (rows, n), 0) < half
    first_core = core[0] == 0
    for block in range(blocks):
        for at in range(tiles):
            other_pairs[at, block] = base_pairs[at, block] - step_len * other[block, at]
    sums = products(other_pairs, [sums_in[at] for at in range(sums_in.shape[0])])

    def total(values):
        return jnp.sum(values, axis=(0, 1), keepdims=True) / pixels

    gram = {}
    at = 0
    for first in range(tiles):
        for second in range(first, tiles):
            direct = [sums[at]]
            at += 1
            if second > first:
                direct.append(sums[at])
                at += 1
            crossed = [sums[at], sums[at + 1]]
            at += 2
            low, high = 2 * first, 2 * second
            gram[low, high] = [total(values[:half]) for values in direct]
            gram[low + 1, high + 1] = [total(values[half:]) for values in direct]
            gram[low, high + 1] = [total(values[:half]) for values in crossed]
            if second > first:
                gram[low + 1, high] = [total(values[half:]) for values in crossed]

    factors = {}
    inverse = []
    for row in range(modes):
        diagonal = gram[row, row][0]
        for inner in range(row):
            real, imag = factors[inner, row]
            diagonal = diagonal - real * real - imag * imag
        inverse.append(lax.rsqrt(diagonal))
        for column in range(row + 1, modes):
            real, imag = gram[row, column]
            for inner in range(row):
                a, b = factors[inner, row]
                c, d = factors[inner, column]
                real = real - (a * c + b * d)
                imag = imag - (a * d - b * c)
            factors[row, column] = (real * inverse[row], imag * inverse[row])

    def apart(block):
        values = []
        for at in range(tiles):
            own, far = own_pairs[at, block], other_pairs[at, block]
            low = jnp.where(first_core, own, far)
            high = jnp.where(first_core, far, own)
            values.append(jnp.where(upper_rows, low, pltpu.roll(high, half, 0)))
            values.append(jnp.where(upper_rows, pltpu.roll(low, half, 0), high))
        return values

    groups = sems.shape[0]
    some = parts // groups
    copies = []
    for group in range(groups):
        for block in range(group * some, (group + 1) * some):
            reals, imags = apart(block), apart(parts + block)
            for mode in range(modes):
                real, imag = reals[mode], imags[mode]
                for inner in range(mode):
                    a, b = factors[inner, mode]
                    real = real - (a * reals[inner] - b * imags[inner])
                    imag = imag - (a * imags[inner] + b * reals[inner])
                reals[mode] = real * inverse[mode]
                imags[mode] = imag * inverse[mode]
                result[mode, 0, block] = reals[mode]
                result[mode, 1, block] = imags[mode]
        here = (slice(None), slice(None), pl.ds(group * some, some))
        copies.append(pltpu.make_async_copy(result.at[here], out.at[here], sems.at[group]))
        copies[-1].start()
    for copy in copies:
        copy.wait()


def shift_pairs(count):
    forward = [(at, at + 1) for at in range(count - 1)]
    return forward, [(target, source) for source, target in forward]


def exchange(values, axis, groups=None):
    return lax.all_to_all(values, axis, 0, 0, tiled=True, axis_index_groups=groups)


def away(values):
    return pltpu.with_memory_space_constraint(values, pltpu.HBM)


def vmem_specs(count):
    return [pl.BlockSpec(memory_space=pltpu.VMEM)] * count


def local(obj_delta, probe_mean, probe_basis, mode_weights, positions, amplitudes):
    n = probe_mean.shape[-1]
    half = n // 2
    modes = probe_basis.shape[0]
    per_tile = positions.shape[2]
    count_y, count_x = lax.axis_size("sy"), lax.axis_size("sx")
    forward_y, backward_y = shift_pairs(count_y)
    forward_x, backward_x = shift_pairs(count_x)
    planes = obj_delta.shape[0] * obj_delta.shape[1]
    blocks = n // 8
    params = pltpu.CompilerParams(vmem_limit_bytes=VMEM_BYTES)
    smem = pl.BlockSpec(memory_space=pltpu.SMEM)

    f32 = jnp.float32
    block = jax.ShapeDtypeStruct((planes, n, n), f32)
    edge = jax.ShapeDtypeStruct((planes, half, n), f32)
    distant = pl.BlockSpec(memory_space=pltpu.HBM)
    upper, lower = pl.pallas_call(
        split_kernel,
        out_shape=(edge, edge),
        in_specs=[distant],
        out_specs=tuple(vmem_specs(2)),
        scratch_shapes=[pltpu.SemaphoreType.DMA((2,))],
        compiler_params=params,
        name="split",
    )(away(obj_delta.reshape(planes, n, n)))
    above = lax.ppermute(lower, "sy", forward_y)
    below = lax.ppermute(upper, "sy", backward_y)
    bf16 = jnp.bfloat16
    probes, forms, measured, packed = pl.pallas_call(
        prepare_kernel,
        out_shape=(
            jax.ShapeDtypeStruct((per_tile, 2, n, n), f32),
            jax.ShapeDtypeStruct((4, 2, 2 * n, 2 * n), bf16),
            jax.ShapeDtypeStruct((per_tile, n, n), f32),
            jax.ShapeDtypeStruct((1, n), f32),
        ),
        in_specs=vmem_specs(1) + [distant] * 5,
        out_specs=tuple(vmem_specs(4)),
        scratch_shapes=[
            pltpu.SMEM((per_tile, modes), f32),
            pltpu.VMEM((2, n, n), f32),
            pltpu.VMEM((modes, 2, n, n), f32),
            pltpu.VMEM((4, 2, n, n), bf16),
            pltpu.SemaphoreType.DMA((5,)),
        ],
        compiler_params=params,
        name="prepare",
    )(
        upper, away(mode_weights[0, 0]), away(probe_mean), away(probe_basis),
        away(amplitudes[0, 0]), away(jnp.asarray(tables(n))),
    )
    above, below, probes, forms, measured, packed = lax.optimization_barrier(
        (above, below, probes, forms, measured, packed)
    )
    to_left, to_right = pl.pallas_call(
        pack_kernel,
        out_shape=(block, block),
        in_specs=vmem_specs(4),
        out_specs=tuple(vmem_specs(2)),
        compiler_params=params,
        name="pack",
    )(upper, lower, above, below)
    from_left = lax.ppermute(to_right, "sx", forward_x)
    from_right = lax.ppermute(to_left, "sx", backward_x)

    probe_grad, terms = pl.pallas_call(
        model_kernel,
        out_shape=(
            jax.ShapeDtypeStruct((4 * blocks * PIECE, 1, n), f32),
            jax.ShapeDtypeStruct((2, per_tile, 2, n, n), f32),
        ),
        in_specs=[distant] + vmem_specs(10),
        out_specs=tuple(vmem_specs(2)),
        scratch_shapes=[
            pltpu.VMEM((planes, 2 * n, 2 * n), f32),
            pltpu.SMEM((per_tile, 2), jnp.int32),
            pltpu.SemaphoreType.DMA(()),
        ],
        compiler_params=params,
        name="model",
    )(
        away(positions[0, 0]), upper, lower, above, below, from_left, from_right,
        probes, forms, measured, packed,
    )
    wide_edge = jax.ShapeDtypeStruct((planes, half, 2 * n), f32)
    up, wide, down = pl.pallas_call(
        deposit_kernel,
        out_shape=(wide_edge, jax.ShapeDtypeStruct((planes, n, 2 * n), f32), wide_edge),
        in_specs=[distant] + vmem_specs(1),
        out_specs=tuple(vmem_specs(3)),
        scratch_shapes=[
            pltpu.VMEM((planes, 2 * n, 2 * n), f32),
            pltpu.SMEM((per_tile, 2), jnp.int32),
            pltpu.SemaphoreType.DMA(()),
        ],
        compiler_params=params,
        name="deposit",
    )(away(positions[0, 0]), terms)

    cores = 2
    per_core = count_x // cores
    columns = [[cores * at + core for at in range(per_core)] for core in range(cores)]
    layers = [
        [row * count_x + cores * at + core for row in range(count_y) for core in range(cores)]
        for at in range(per_core)
    ]
    gathered = exchange(probe_grad, ("sy", "sx"), layers)
    parts = pl.pallas_call(
        mix_kernel,
        out_shape=jax.ShapeDtypeStruct((per_core, modes // 2, 8, n), f32),
        in_specs=vmem_specs(1),
        out_specs=vmem_specs(1)[0],
        scratch_shapes=[pltpu.VMEM((4 * modes, n), f32)],
        compiler_params=params,
        name="mix",
    )(gathered)
    parts = exchange(parts, "sx", columns)
    from_below = lax.ppermute(up, "sy", backward_y)
    from_above = lax.ppermute(down, "sy", forward_y)
    parts = pl.pallas_call(
        repeat_kernel,
        out_shape=jax.ShapeDtypeStruct((count_y,) + parts.shape[1:], f32),
        in_specs=vmem_specs(1),
        out_specs=vmem_specs(1)[0],
        compiler_params=params,
        name="repeat",
    )(parts)
    parts, from_below, from_above = lax.optimization_barrier((parts, from_below, from_above))
    middle, to_left, to_right = pl.pallas_call(
        merge_kernel,
        out_shape=(block, edge, edge),
        in_specs=vmem_specs(3),
        out_specs=tuple(vmem_specs(3)),
        compiler_params=params,
        name="merge",
    )(wide, from_above, from_below)
    mine = exchange(parts, "sy")
    from_left = lax.ppermute(to_right, "sx", forward_x)
    from_right = lax.ppermute(to_left, "sx", backward_x)
    mine, from_left, from_right = lax.optimization_barrier((mine, from_left, from_right))
    obj_grad = pl.pallas_call(
        finish_kernel,
        out_shape=block,
        in_specs=vmem_specs(3),
        out_specs=vmem_specs(1)[0],
        compiler_params=params,
        name="finish",
    )(middle, from_left, from_right)
    swap = [(at, at ^ 1) for at in range(count_x)]
    other = lax.ppermute(mine, "sx", swap)
    other, obj_grad = lax.optimization_barrier((other, obj_grad))
    core = (lax.axis_index("sx") % cores).astype(jnp.int32).reshape(1)
    count_all = per_tile * count_y * count_x
    step_len = 1.0 / math.sqrt(count_all)

    tiles = modes // 2
    pair_shape = (tiles, 2 * blocks, 8, n)
    sum_count = 2 * tiles * tiles + tiles
    own_pairs, base_pairs, sums = pl.pallas_call(
        functools.partial(own_kernel, step_len=step_len),
        out_shape=(
            jax.ShapeDtypeStruct(pair_shape, f32),
            jax.ShapeDtypeStruct(pair_shape, f32),
            jax.ShapeDtypeStruct((sum_count, 8, n), f32),
        ),
        in_specs=[smem] + vmem_specs(2),
        out_specs=tuple(vmem_specs(3)),
        compiler_params=params,
        name="own_half",
    )(core, mine, probe_basis.reshape(modes, 2 * blocks, 8, n))
    new_basis = pl.pallas_call(
        functools.partial(ortho_kernel, step_len=step_len),
        out_shape=jax.ShapeDtypeStruct((modes, 2, blocks, 8, n), f32),
        in_specs=[smem] + vmem_specs(4),
        out_specs=distant,
        scratch_shapes=[
            pltpu.VMEM(pair_shape, f32),
            pltpu.VMEM((modes, 2, blocks, 8, n), f32),
            pltpu.SemaphoreType.DMA((4,)),
        ],
        compiler_params=params,
        name="orthonormal",
    )(core, other, own_pairs, base_pairs, sums)
    new_basis = new_basis.reshape(probe_basis.shape)
    return (obj_grad.reshape(obj_delta.shape), new_basis)


def solution(mesh):
    placed = (
        P(None, None, "sy", "sx"),
        P(),
        P(),
        P("sy", "sx", None, None),
        P("sy", "sx", None, None),
        P("sy", "sx", None, None, None),
    )
    return jax.shard_map(
        local,
        mesh=mesh,
        in_specs=placed,
        out_specs=(P(None, None, "sy", "sx"), P()),
        check_vma=False,
    )
```

```python
import functools
import math

import jax
import jax.numpy as jnp
import numpy as np
from jax import lax
from jax.experimental import pallas as pl
from jax.experimental.pallas import tpu as pltpu
from jax.sharding import PartitionSpec as P

FLOOR = 0.5
PHASE_EDGE = 3.0
VMEM_BYTES = 40 * 1024 * 1024
PIECE = 9


def split_table(values):
    whole = values.astype(np.float32)
    high = whole.astype(jnp.bfloat16)
    low = (whole - high.astype(np.float32)).astype(jnp.bfloat16)
    return np.stack([high, low])


def tables(probe_len):
    indices = np.arange(probe_len)
    dft = np.exp(-2j * np.pi * (np.outer(indices, indices) % probe_len) / probe_len)
    dft = dft / math.sqrt(probe_len)
    half = probe_len // 2
    frequency = ((indices + half) % probe_len - half) / half
    phase = np.exp(-1j * PHASE_EDGE * frequency * frequency)
    move = np.conj(dft) @ (phase[:, None] * dft)
    parts = [split_table(part) for form in (dft, move) for part in (form.real, form.imag)]
    return np.stack(parts)


def block_forms(real, imag):
    above = jnp.concatenate([real, -imag], axis=1)
    below = jnp.concatenate([imag, real], axis=1)
    above_t = jnp.concatenate([real, imag], axis=1)
    below_t = jnp.concatenate([-imag, real], axis=1)
    return (
        jnp.concatenate([above, below], axis=0),
        jnp.concatenate([above_t, below_t], axis=0),
    )


def dot3(left, right):
    left_high, left_low = left
    right_high, right_low = right
    return jnp.dot(
        jnp.concatenate([left_high, left_low, left_high], axis=1),
        jnp.concatenate([right_low, right_high, right_high], axis=0),
        preferred_element_type=jnp.float32,
    )


def halves(values):
    high = values.astype(jnp.bfloat16)
    low = (values - high.astype(jnp.float32)).astype(jnp.bfloat16)
    return (high, low)


def both_sides(fields, left_table, right_table):
    (real0, imag0), (real1, imag1) = fields
    n = real0.shape[0]
    upright = jnp.concatenate(
        [jnp.concatenate([real0, real1], axis=1), jnp.concatenate([imag0, imag1], axis=1)], axis=0
    )
    upright = dot3(left_table, halves(upright))
    top, bottom = upright[:n], upright[n:]
    wide = jnp.concatenate(
        [
            jnp.concatenate([top[:, :n], bottom[:, :n]], axis=1),
            jnp.concatenate([top[:, n:], bottom[:, n:]], axis=1),
        ],
        axis=0,
    )
    wide = dot3(halves(wide), right_table)
    return [(wide[:n, :n], wide[:n, n:]), (wide[n:, :n], wide[n:, n:])]


def near_lanes(shape):
    return lax.broadcasted_iota(jnp.int32, shape, len(shape) - 1) < shape[-1] // 2


def roll_planes(values):
    return jnp.stack([pltpu.roll(plane, plane.shape[-1] // 2, 1) for plane in values])


def split_kernel(source, upper, lower, sems):
    half = upper.shape[1]
    copies = [
        pltpu.make_async_copy(source.at[:, 0:half], upper, sems.at[0]),
        pltpu.make_async_copy(source.at[:, half : 2 * half], lower, sems.at[1]),
    ]
    for copy in copies:
        copy.start()
    for copy in copies:
        copy.wait()


def spread(several, out, sems):
    some = several.shape[0]
    copies = [
        pltpu.make_async_copy(several, out.at[pl.ds(at * some, some)], sems.at[at])
        for at in range(sems.shape[0])
    ]
    for copy in copies:
        copy.start()
    for copy in copies:
        copy.wait()


def repeat_kernel(parts, out, several, sems):
    total = parts[0]
    for at in range(1, parts.shape[0]):
        total = total + parts[at]
    for at in range(several.shape[0]):
        several[at] = total
    spread(several, out, sems)


def pack_kernel(upper, lower, above, below, to_left, to_right):
    near = near_lanes(to_left.shape)
    first = jnp.concatenate([above[...], upper[...]], axis=1)
    second = jnp.concatenate([lower[...], below[...]], axis=1)
    second = roll_planes(second)
    to_left[...] = jnp.where(near, first, second)
    to_right[...] = jnp.where(near, second, first)


def merge_kernel(wide, from_above, from_below, middle, to_left, to_right):
    n = middle.shape[-1]
    half = n // 2
    upper = wide[:, :half] + from_above[...]
    lower = wide[:, half:] + from_below[...]
    middle[:, :half] = upper[:, :, :n]
    middle[:, half:] = lower[:, :, :n]
    first = upper[:, :, n:]
    second = roll_planes(lower[:, :, n:])
    near = near_lanes(first.shape)
    to_right[...] = jnp.where(near, first, second)
    to_left[...] = jnp.where(near, second, first)


def finish_kernel(middle, from_left, from_right, out):
    half = middle.shape[1] // 2
    near = near_lanes(from_left.shape)
    left, right = from_left[...], from_right[...]
    out[:, :half] = middle[:, :half] + jnp.where(near, left, right)
    out[:, half:] = middle[:, half:] + roll_planes(jnp.where(near, right, left))


def prepare_kernel(
    after, weights_in, mean_in, basis_in, measured_in, table_in,
    probes, forms, measured, packed, weights, mean, basis, table, sems,
):
    del after
    copies = [
        pltpu.make_async_copy(source, target, sems.at[at])
        for at, (source, target) in enumerate(
            [
                (weights_in, weights),
                (table_in, table),
                (mean_in, mean),
                (basis_in, basis),
                (measured_in, measured),
            ]
        )
    ]
    for copy in copies:
        copy.start()
    n = mean.shape[-1]
    modes = basis.shape[0]
    slots = range(2)
    copies[0].wait()
    lane_at = lax.broadcasted_iota(jnp.int32, (1, n), 1)
    row = jnp.zeros((1, n), jnp.float32)
    for slot in slots:
        for mode in range(modes):
            row = jnp.where(lane_at == slot * modes + mode, weights[slot, mode], row)
    packed[...] = row
    copies[1].wait()
    for at in range(2):
        for part in range(2):
            form, form_t = block_forms(table[2 * at, part], table[2 * at + 1, part])
            forms[2 * at, part] = form
            forms[2 * at + 1, part] = form_t
    copies[2].wait()
    copies[3].wait()
    for slot in slots:
        real = mean[0]
        imag = mean[1]
        for mode in range(modes):
            real = real + weights[slot, mode] * basis[mode, 0]
            imag = imag + weights[slot, mode] * basis[mode, 1]
        probes[slot, 0] = real
        probes[slot, 1] = imag
    copies[4].wait()


def model_kernel(
    positions_in, upper, lower, above, below, from_left, from_right, probes_in, forms, measured, packed,
    probe_grad, terms, frame, positions, sem,
):
    copy = pltpu.make_async_copy(positions_in, positions, sem)
    copy.start()
    n = measured.shape[-1]
    half = n // 2
    near = near_lanes(from_left.shape)
    frame[:, 0:half, 0:n] = above[...]
    frame[:, half:n, 0:n] = upper[...]
    frame[:, n : n + half, 0:n] = lower[...]
    frame[:, half + n : 2 * n, 0:n] = below[...]
    frame[:, 0:n, n : 2 * n] = jnp.where(near, from_right[...], from_left[...])
    frame[:, n : 2 * n, n : 2 * n] = roll_planes(
        jnp.where(near, from_left[...], from_right[...])
    )
    slots = range(2)
    copy.wait()
    rows = [positions[slot, 0] for slot in slots]
    cols = [positions[slot, 1] for slot in slots]
    offsets = [row & 7 for row in rows]
    bases = [pl.multiple_of(row - offset, 8) for row, offset in zip(rows, offsets)]
    span = n + 8

    def window(slot, plane):
        strip = frame[plane, pl.ds(bases[slot], span), :]
        strip = pltpu.roll(strip, (5 * half - cols[slot]) & (2 * n - 1), 1)[:, :n]
        shift = jnp.where(offsets[slot] == 0, 0, span - offsets[slot])
        return pltpu.roll(strip, shift, 0)[:n]

    transmit = [
        [(1.0 + window(slot, 2 * layer), window(slot, 2 * layer + 1)) for slot in slots]
        for layer in range(2)
    ]
    probes = [(probes_in[slot, 0], probes_in[slot, 1]) for slot in slots]
    dft, dft_t, move, move_t = [(forms[at, 0], forms[at, 1]) for at in range(4)]

    def times(first, second):
        return [(a * c - b * d, a * d + b * c) for (a, b), (c, d) in zip(first, second)]

    def conj_times(first, second):
        return [(a * c + b * d, a * d - b * c) for (a, b), (c, d) in zip(first, second)]

    def keep(layer, pairs):
        for slot in slots:
            for part in range(2):
                terms[layer, slot, part] = pairs[slot][part]

    entered = both_sides(times(probes, transmit[0]), move, move_t)
    far = both_sides(times(entered, transmit[1]), dft, dft_t)
    chi = []
    for slot in slots:
        real, imag = far[slot]
        inverse = jnp.minimum(lax.rsqrt(real * real + imag * imag), 1.0 / FLOOR)
        ratio = measured[slot] * inverse
        chi.append((real - real * ratio, imag - imag * ratio))
    back = both_sides(chi, dft_t, dft)
    keep(1, conj_times(entered, back))
    back = both_sides(conj_times(transmit[1], back), move_t, move)
    keep(0, conj_times(probes, back))
    back = conj_times(transmit[0], back)
    blocks = n // 8
    upper_rows = lax.broadcasted_iota(jnp.int32, (8, n), 0) < 4
    for part in range(2):
        for block in range(blocks):
            first = back[0][part][8 * block : 8 * block + 8]
            second = back[1][part][8 * block : 8 * block + 8]
            at = 2 * PIECE * (part * blocks + block)
            probe_grad[pl.ds(at, 8), 0, :] = jnp.where(
                upper_rows, first, pltpu.roll(second, 4, 0)
            )
            probe_grad[at + 8] = packed[...]
            probe_grad[pl.ds(at + PIECE, 8), 0, :] = jnp.where(
                upper_rows, pltpu.roll(first, 4, 0), second
            )
            probe_grad[at + PIECE + 8] = packed[...]


def deposit_kernel(positions_in, terms, up, wide, down, grads, positions, sem):
    copy = pltpu.make_async_copy(positions_in, positions, sem)
    copy.start()
    n = terms.shape[-1]
    half = n // 2
    span = n + 8
    grads[...] = jnp.zeros(grads.shape, jnp.float32)
    copy.wait()
    for slot in range(2):
        row, col = positions[slot, 0], positions[slot, 1]
        offset = row & 7
        base = pl.multiple_of(row - offset, 8)
        for plane in range(4):
            padded = jnp.concatenate(
                [terms[plane // 2, slot, plane % 2], jnp.zeros((8, n), jnp.float32)], axis=0
            )
            lowered = pltpu.roll(padded, offset, 0)
            padded = jnp.concatenate([lowered, jnp.zeros((span, n), jnp.float32)], axis=1)
            shifted = pltpu.roll(padded, (col + 3 * half) & (2 * n - 1), 1)
            at = (plane, pl.ds(base, span), slice(None))
            grads[at] = grads[at] + shifted
    up[...] = grads[:, 0:half]
    wide[...] = grads[:, half : half + n]
    down[...] = grads[:, half + n : 2 * n]


def mix_kernel(gathered, out, ordered, several, sems):
    copies, pairs, rows, n = several.shape
    modes = 2 * pairs
    some = rows // 2
    count = gathered.shape[0] // PIECE

    def row_of_all(at):
        return gathered[pl.ds(at, count, stride=PIECE), 0, :]

    factors = row_of_all(rows).T[: 2 * modes]
    terms = jnp.concatenate([row_of_all(at) for at in range(rows)], axis=1)
    product = jnp.dot(
        factors, terms, precision=lax.Precision.HIGHEST, preferred_element_type=jnp.float32
    )
    for row in range(some):
        first = product[:modes, row * n : (row + 1) * n]
        second = product[modes:, (some + row) * n : (some + row + 1) * n]
        ordered[pl.ds(row, modes, stride=some), :] = first + second
    for pair in range(pairs):
        tile = ordered[pair * rows : (pair + 1) * rows]
        for copy in range(copies):
            several[copy, pair] = tile
    spread(several, out, sems)


def products(pairs, sums):
    tiles, blocks, rows = pairs.shape[0], pairs.shape[1], pairs.shape[2]
    parts = blocks // 2
    sums = list(sums)
    for block in range(parts):
        real = [pairs[at, block] for at in range(tiles)]
        imag = [pairs[at, parts + block] for at in range(tiles)]
        turned_real = [pltpu.roll(values, rows // 2, 0) for values in real]
        turned_imag = [pltpu.roll(values, rows // 2, 0) for values in imag]
        at = 0
        for first in range(tiles):
            a, b = real[first], imag[first]
            for second in range(first, tiles):
                c, d = real[second], imag[second]
                sums[at] = sums[at] + (a * c + b * d)
                at += 1
                if second > first:
                    sums[at] = sums[at] + (a * d - b * c)
                    at += 1
                c, d = turned_real[second], turned_imag[second]
                sums[at] = sums[at] + (a * c + b * d)
                sums[at + 1] = sums[at + 1] + (a * d - b * c)
                at += 2
    return sums


def own_kernel(core, mine, basis, own_pairs, base_pairs, sums_out, step_len=None):
    tiles, blocks, rows, n = own_pairs.shape
    upper_rows = lax.broadcasted_iota(jnp.int32, (rows, n), 0) < rows // 2
    first_core = core[0] == 0
    for block in range(blocks):
        for at in range(tiles):
            even, odd = basis[2 * at, block], basis[2 * at + 1, block]
            low = jnp.where(upper_rows, even, pltpu.roll(odd, rows // 2, 0))
            high = jnp.where(upper_rows, pltpu.roll(even, rows // 2, 0), odd)
            base = jnp.where(first_core, low, high)
            own_pairs[at, block] = base - step_len * mine[block, at]
            base_pairs[at, block] = jnp.where(first_core, high, low)
    zero = jnp.zeros((rows, n), jnp.float32)
    sums = products(own_pairs, [zero] * sums_out.shape[0])
    for at, values in enumerate(sums):
        sums_out[at] = values


def ortho_kernel(
    core, other, own_pairs, base_pairs, sums_in, out, other_pairs, result, sems, step_len=None
):
    tiles, blocks, rows, n = own_pairs.shape
    modes = 2 * tiles
    parts = blocks // 2
    pixels = parts * rows * n
    half = rows // 2
    upper_rows = lax.broadcasted_iota(jnp.int32, (rows, n), 0) < half
    first_core = core[0] == 0
    for block in range(blocks):
        for at in range(tiles):
            other_pairs[at, block] = base_pairs[at, block] - step_len * other[block, at]
    sums = products(other_pairs, [sums_in[at] for at in range(sums_in.shape[0])])

    def total(values):
        return jnp.sum(values, axis=(0, 1), keepdims=True) * (1.0 / pixels)

    gram = {}
    at = 0
    for first in range(tiles):
        for second in range(first, tiles):
            direct = [sums[at]]
            at += 1
            if second > first:
                direct.append(sums[at])
                at += 1
            crossed = [sums[at], sums[at + 1]]
            at += 2
            low, high = 2 * first, 2 * second
            gram[low, high] = [total(values[:half]) for values in direct]
            gram[low + 1, high + 1] = [total(values[half:]) for values in direct]
            gram[low, high + 1] = [total(values[:half]) for values in crossed]
            if second > first:
                gram[low + 1, high] = [total(values[half:]) for values in crossed]

    factors = {}
    inverse = []
    for row in range(modes):
        diagonal = gram[row, row][0]
        for inner in range(row):
            real, imag = factors[inner, row]
            diagonal = diagonal - real * real - imag * imag
        inverse.append(lax.rsqrt(diagonal))
        for column in range(row + 1, modes):
            real, imag = gram[row, column]
            for inner in range(row):
                a, b = factors[inner, row]
                c, d = factors[inner, column]
                real = real - (a * c + b * d)
                imag = imag - (a * d - b * c)
            factors[row, column] = (real * inverse[row], imag * inverse[row])

    def apart(block):
        values = []
        for at in range(tiles):
            own, far = own_pairs[at, block], other_pairs[at, block]
            low = jnp.where(first_core, own, far)
            high = jnp.where(first_core, far, own)
            values.append(jnp.where(upper_rows, low, pltpu.roll(high, half, 0)))
            values.append(jnp.where(upper_rows, pltpu.roll(low, half, 0), high))
        return values

    groups = sems.shape[0]
    some = parts // groups
    copies = []
    for group in range(groups):
        for block in range(group * some, (group + 1) * some):
            reals, imags = apart(block), apart(parts + block)
            for mode in range(modes):
                real, imag = reals[mode], imags[mode]
                for inner in range(mode):
                    a, b = factors[inner, mode]
                    real = real - (a * reals[inner] - b * imags[inner])
                    imag = imag - (a * imags[inner] + b * reals[inner])
                reals[mode] = real * inverse[mode]
                imags[mode] = imag * inverse[mode]
                result[mode, 0, block] = reals[mode]
                result[mode, 1, block] = imags[mode]
        here = (slice(None), slice(None), pl.ds(group * some, some))
        copies.append(pltpu.make_async_copy(result.at[here], out.at[here], sems.at[group]))
        copies[-1].start()
    for copy in copies:
        copy.wait()


def shift_pairs(count):
    forward = [(at, at + 1) for at in range(count - 1)]
    return forward, [(target, source) for source, target in forward]


def exchange(values, axis, groups=None):
    return lax.all_to_all(values, axis, 0, 0, tiled=True, axis_index_groups=groups)


def away(values):
    return pltpu.with_memory_space_constraint(values, pltpu.HBM)


def vmem_specs(count):
    return [pl.BlockSpec(memory_space=pltpu.VMEM)] * count


def local(obj_delta, probe_mean, probe_basis, mode_weights, positions, amplitudes):
    n = probe_mean.shape[-1]
    half = n // 2
    modes = probe_basis.shape[0]
    per_tile = positions.shape[2]
    count_y, count_x = lax.axis_size("sy"), lax.axis_size("sx")
    forward_y, backward_y = shift_pairs(count_y)
    forward_x, backward_x = shift_pairs(count_x)
    planes = obj_delta.shape[0] * obj_delta.shape[1]
    blocks = n // 8
    params = pltpu.CompilerParams(vmem_limit_bytes=VMEM_BYTES)
    smem = pl.BlockSpec(memory_space=pltpu.SMEM)

    f32 = jnp.float32
    block = jax.ShapeDtypeStruct((planes, n, n), f32)
    edge = jax.ShapeDtypeStruct((planes, half, n), f32)
    distant = pl.BlockSpec(memory_space=pltpu.HBM)
    upper, lower = pl.pallas_call(
        split_kernel,
        out_shape=(edge, edge),
        in_specs=[distant],
        out_specs=tuple(vmem_specs(2)),
        scratch_shapes=[pltpu.SemaphoreType.DMA((2,))],
        compiler_params=params,
        name="split",
    )(away(obj_delta.reshape(planes, n, n)))
    above = lax.ppermute(lower, "sy", forward_y)
    below = lax.ppermute(upper, "sy", backward_y)
    bf16 = jnp.bfloat16
    probes, forms, measured, packed = pl.pallas_call(
        prepare_kernel,
        out_shape=(
            jax.ShapeDtypeStruct((per_tile, 2, n, n), f32),
            jax.ShapeDtypeStruct((4, 2, 2 * n, 2 * n), bf16),
            jax.ShapeDtypeStruct((per_tile, n, n), f32),
            jax.ShapeDtypeStruct((1, n), f32),
        ),
        in_specs=vmem_specs(1) + [distant] * 5,
        out_specs=tuple(vmem_specs(4)),
        scratch_shapes=[
            pltpu.SMEM((per_tile, modes), f32),
            pltpu.VMEM((2, n, n), f32),
            pltpu.VMEM((modes, 2, n, n), f32),
            pltpu.VMEM((4, 2, n, n), bf16),
            pltpu.SemaphoreType.DMA((5,)),
        ],
        compiler_params=params,
        name="prepare",
    )(
        upper, away(mode_weights[0, 0]), away(probe_mean), away(probe_basis),
        away(amplitudes[0, 0]), away(jnp.asarray(tables(n))),
    )
    above, below, probes, forms, measured, packed = lax.optimization_barrier(
        (above, below, probes, forms, measured, packed)
    )
    to_left, to_right = pl.pallas_call(
        pack_kernel,
        out_shape=(block, block),
        in_specs=vmem_specs(4),
        out_specs=tuple(vmem_specs(2)),
        compiler_params=params,
        name="pack",
    )(upper, lower, above, below)
    from_left = lax.ppermute(to_right, "sx", forward_x)
    from_right = lax.ppermute(to_left, "sx", backward_x)

    probe_grad, terms = pl.pallas_call(
        model_kernel,
        out_shape=(
            jax.ShapeDtypeStruct((4 * blocks * PIECE, 1, n), f32),
            jax.ShapeDtypeStruct((2, per_tile, 2, n, n), f32),
        ),
        in_specs=[distant] + vmem_specs(10),
        out_specs=tuple(vmem_specs(2)),
        scratch_shapes=[
            pltpu.VMEM((planes, 2 * n, 2 * n), f32),
            pltpu.SMEM((per_tile, 2), jnp.int32),
            pltpu.SemaphoreType.DMA(()),
        ],
        compiler_params=params,
        name="model",
    )(
        away(positions[0, 0]), upper, lower, above, below, from_left, from_right,
        probes, forms, measured, packed,
    )
    wide_edge = jax.ShapeDtypeStruct((planes, half, 2 * n), f32)
    up, wide, down = pl.pallas_call(
        deposit_kernel,
        out_shape=(wide_edge, jax.ShapeDtypeStruct((planes, n, 2 * n), f32), wide_edge),
        in_specs=[distant] + vmem_specs(1),
        out_specs=tuple(vmem_specs(3)),
        scratch_shapes=[
            pltpu.VMEM((planes, 2 * n, 2 * n), f32),
            pltpu.SMEM((per_tile, 2), jnp.int32),
            pltpu.SemaphoreType.DMA(()),
        ],
        compiler_params=params,
        name="deposit",
    )(away(positions[0, 0]), terms)

    cores = 2
    per_core = count_x // cores
    columns = [[cores * at + core for at in range(per_core)] for core in range(cores)]
    layers = [
        [row * count_x + cores * at + core for row in range(count_y) for core in range(cores)]
        for at in range(per_core)
    ]
    gathered = exchange(probe_grad, ("sy", "sx"), layers)
    parts = pl.pallas_call(
        mix_kernel,
        out_shape=jax.ShapeDtypeStruct((per_core, modes // 2, 8, n), f32),
        in_specs=vmem_specs(1),
        out_specs=distant,
        scratch_shapes=[
            pltpu.VMEM((4 * modes, n), f32),
            pltpu.VMEM((per_core // 4, modes // 2, 8, n), f32),
            pltpu.SemaphoreType.DMA((4,)),
        ],
        compiler_params=params,
        name="mix",
    )(gathered)
    parts = exchange(parts, "sx", columns)
    from_below = lax.ppermute(up, "sy", backward_y)
    from_above = lax.ppermute(down, "sy", forward_y)
    parts = pl.pallas_call(
        repeat_kernel,
        out_shape=jax.ShapeDtypeStruct((count_y,) + parts.shape[1:], f32),
        in_specs=vmem_specs(1),
        out_specs=distant,
        scratch_shapes=[
            pltpu.VMEM((count_y // 4,) + parts.shape[1:], f32),
            pltpu.SemaphoreType.DMA((4,)),
        ],
        compiler_params=params,
        name="repeat",
    )(parts)
    parts, from_below, from_above = lax.optimization_barrier((parts, from_below, from_above))
    middle, to_left, to_right = pl.pallas_call(
        merge_kernel,
        out_shape=(block, edge, edge),
        in_specs=vmem_specs(3),
        out_specs=tuple(vmem_specs(3)),
        compiler_params=params,
        name="merge",
    )(wide, from_above, from_below)
    mine = exchange(parts, "sy")
    from_left = lax.ppermute(to_right, "sx", forward_x)
    from_right = lax.ppermute(to_left, "sx", backward_x)
    mine, from_left, from_right = lax.optimization_barrier((mine, from_left, from_right))
    obj_grad = pl.pallas_call(
        finish_kernel,
        out_shape=block,
        in_specs=vmem_specs(3),
        out_specs=vmem_specs(1)[0],
        compiler_params=params,
        name="finish",
    )(middle, from_left, from_right)
    swap = [(at, at ^ 1) for at in range(count_x)]
    other = lax.ppermute(mine, "sx", swap)
    other, obj_grad = lax.optimization_barrier((other, obj_grad))
    core = (lax.axis_index("sx") % cores).astype(jnp.int32).reshape(1)
    count_all = per_tile * count_y * count_x
    step_len = 1.0 / math.sqrt(count_all)

    tiles = modes // 2
    pair_shape = (tiles, 2 * blocks, 8, n)
    sum_count = 2 * tiles * tiles + tiles
    own_pairs, base_pairs, sums = pl.pallas_call(
        functools.partial(own_kernel, step_len=step_len),
        out_shape=(
            jax.ShapeDtypeStruct(pair_shape, f32),
            jax.ShapeDtypeStruct(pair_shape, f32),
            jax.ShapeDtypeStruct((sum_count, 8, n), f32),
        ),
        in_specs=[smem] + vmem_specs(2),
        out_specs=tuple(vmem_specs(3)),
        compiler_params=params,
        name="own_half",
    )(core, mine, probe_basis.reshape(modes, 2 * blocks, 8, n))
    new_basis = pl.pallas_call(
        functools.partial(ortho_kernel, step_len=step_len),
        out_shape=jax.ShapeDtypeStruct((modes, 2, blocks, 8, n), f32),
        in_specs=[smem] + vmem_specs(4),
        out_specs=distant,
        scratch_shapes=[
            pltpu.VMEM(pair_shape, f32),
            pltpu.VMEM((modes, 2, blocks, 8, n), f32),
            pltpu.SemaphoreType.DMA((4,)),
        ],
        compiler_params=params,
        name="orthonormal",
    )(core, other, own_pairs, base_pairs, sums)
    new_basis = new_basis.reshape(probe_basis.shape)
    return (obj_grad.reshape(obj_delta.shape), new_basis)


def solution(mesh):
    placed = (
        P(None, None, "sy", "sx"),
        P(),
        P(),
        P("sy", "sx", None, None),
        P("sy", "sx", None, None),
        P("sy", "sx", None, None, None),
    )
    return jax.shard_map(
        local,
        mesh=mesh,
        in_specs=placed,
        out_specs=(P(None, None, "sy", "sx"), P()),
        check_vma=False,
    )
```
